512 devices in a mesh: dp: 64 (over y, z), mp: 8 (over x, core).
Axes of the slice: x: 4, y: 4, z: 16, core: 2. Of those that a mesh axis runs over, the one named last changes fastest.
Arguments:
- preact: float32 [64, 16, 16, 1024], P('dp', None, None, 'mp'), may hold values from -6 to 6
- weights: float32 [512, 9, 1024], P('mp'), may hold values from -0.0625 to 0.0625
- cotangent: float32 [64, 16, 16, 512], P('dp', None, None, 'mp'), may hold values from -24 to 24
Outputs:
- output: float32 [64, 16, 16, 512], P('dp', None, None, 'mp')
- input_grad: float32 [64, 16, 16, 1024], P('dp', None, None, 'mp')
- weight_grad: float32 [512, 9216], P('mp', 'dp')
The draws below stay inside these ranges and needn't reach their ends.
All inputs are finite; a program needn't handle non-finite values.
Results may differ from the reference program's by a relative error of at most 0.0003.
Values sent between devices are 32-bit elements; how exact they have to be, the bound alone decides.
A program may use at most 64 MiB of HBM per device.

```python
import jax
import jax.numpy as jnp
from jax import lax

CIN = 1024
COUT = 512
SIDE = 16
IMG_DEV = 1
IMAGES = 64
N_DP = 64


def draw_cotangent(key, part):
    shared = jax.random.normal(jax.random.fold_in(key, 101), (SIDE, SIDE, COUT), jnp.float32)
    progress = jnp.arange(IMAGES, dtype=jnp.float32) / max(IMAGES - 1, 1)
    jitter = jax.random.uniform(jax.random.fold_in(key, 103), (IMAGES,), jnp.float32, 0.8, 1.25)
    channel_scale = jnp.exp(jax.random.uniform(jax.random.fold_in(key, 104), (COUT,), jnp.float32, -1.2, 1.2))
    fluctuation = jax.random.normal(jax.random.fold_in(key, 102), (IMAGES, SIDE, SIDE, COUT), jnp.float32)
    image_scale = 3.0 ** progress * jitter
    drawn = image_scale[:, None, None, None] * channel_scale * (0.7 * shared + 0.7 * fluctuation)
    return jnp.clip(drawn, -24.0, 24.0)


def block_scale(stream_key, dims, split, least, largest):
    def one(axis_at, blocks):
        draws = jax.random.uniform(jax.random.fold_in(jax.random.fold_in(stream_key, 6), axis_at), (blocks,), jnp.float32, least / len(split), largest / len(split))
        return jnp.repeat(jnp.exp(draws), dims[axis_at] // blocks).reshape((-1,) + (1,) * (len(dims) - axis_at - 1))

    loudness = one(*split[0])
    for cut in split[1:]:
        loudness = loudness * one(*cut)
    return loudness


def gaussian(own_key, dims, scale, bound, shards=(), kind=jnp.bfloat16):
    factor_of = block_scale(own_key, dims, shards, -0.22, 0.18) if shards else 1.0
    array = jax.random.normal(own_key, dims, jnp.float32) * scale * factor_of
    return jnp.minimum(jnp.maximum(array, -bound), bound).astype(kind)


def setup_inputs(seed: int = 0) -> dict:
    streams_of = jax.random.split(jax.random.key(seed), 4)
    return {
        "preact": gaussian(streams_of[0], (IMAGES, SIDE, SIDE, CIN), 1.0, 6.0, ((0, 64), (3, 8)), jnp.float32),
        "weights": gaussian(streams_of[1], (COUT, 9, CIN), (9 * CIN) ** -0.5, 0.0625, ((0, 8),), jnp.float32),
        "cotangent": draw_cotangent(jax.random.fold_in(streams_of[3], 71), 0),
    }


highest = lax.Precision.HIGHEST
epsilon = 1e-06

def activate(values):
    return 0.5 * values * (1.0 + lax.erf(values * 0.7071067811865476))

def gelu_slope(values):
    return 0.5 * (1.0 + lax.erf(values * 0.7071067811865476)) + values * jnp.exp(-0.5 * values * values) * 0.3989422804014327

def convolve(activity, filters):
    kernel = filters.reshape(filters.shape[0], 3, 3, filters.shape[2]).transpose(1, 2, 3, 0)
    return lax.conv_general_dilated(activity, kernel, (1, 1), 'SAME', dimension_numbers=('NHWC', 'HWIO', 'NHWC'), precision=highest)

def adasum(leading, second):
    cross = jnp.sum(leading * second)
    lead_sq = jnp.sum(leading * leading)
    second_sq = jnp.sum(second * second)
    return (1.0 - cross / (2.0 * (lead_sq + epsilon))) * leading + (1.0 - cross / (2.0 * (second_sq + epsilon))) * second

def reference(preact, weights, cotangent):
    activated = activate(preact)
    output = convolve(activated, weights)
    unused, pullback = jax.vjp(lambda activity: convolve(activity, weights), activated)
    input_grad = pullback(cotangent)[0] * gelu_slope(preact)

    def leaf_grad(position):
        begin = (position * IMG_DEV).astype(jnp.int32)
        activity = lax.dynamic_slice_in_dim(activated, begin, IMG_DEV, 0)
        upstream = lax.dynamic_slice_in_dim(cotangent, begin, IMG_DEV, 0)
        unused_out, pull_leaf = jax.vjp(lambda filters: convolve(activity, filters), weights)
        return pull_leaf(upstream)[0] / float(IMG_DEV * SIDE * SIDE)

    def pair_grad(position):
        return adasum(leaf_grad(2 * position), leaf_grad(2 * position + 1))
    stacked = lax.map(pair_grad, jnp.arange(N_DP // 2, dtype=jnp.int32))
    while stacked.shape[0] > 1:
        halves = stacked.reshape((stacked.shape[0] // 2, 2) + stacked.shape[1:])
        stacked = jax.vmap(adasum)(halves[:, 0], halves[:, 1])
    weight_grad = stacked[0].reshape(COUT, 9 * CIN)
    return (output, input_grad, weight_grad)
```

```python
import functools

import jax
import jax.numpy as jnp
from jax import lax
from jax.experimental import pallas as pl
from jax.experimental.pallas import tpu as pltpu
from jax.sharding import PartitionSpec as P

MESH = pl.DeviceIdType.MESH
F32 = jnp.float32
BF16 = jnp.bfloat16
EPS = 1e-06
SIDE = 16
PIX = SIDE * SIDE
TAPS = 9
STACK = 640


def halves(values):
    high = values.astype(BF16)
    low = (values - high.astype(F32)).astype(BF16)
    return high, low


def dot3(a, b, dims):
    one = lambda p, q: lax.dot_general(p, q, (dims, ((), ())), preferred_element_type=F32)
    return one(a[0], b[0]) + (one(a[0], b[1]) + one(a[1], b[0]))


NN = ((1,), (0,))
NT = ((1,), (1,))


def shifted(values, dy, dx):
    pixel = lax.broadcasted_iota(jnp.int32, values.shape, 1)
    column = jnp.bitwise_and(pixel, SIDE - 1)
    inside = None
    if dx:
        inside = (column >= 1) if dx < 0 else (column < SIDE - 1)
    if dy:
        rows = (pixel >= SIDE) if dy < 0 else (pixel < PIX - SIDE)
        inside = rows if inside is None else jnp.logical_and(inside, rows)
    step = SIDE * dy + dx
    if step == 0:
        return values
    return jnp.where(inside, pltpu.roll(values, (-step) % PIX, 1), 0.0)


def stacked_taps(cot):
    taps = [shifted(cot, 1 - t // 3, 1 - t % 3) for t in range(TAPS)]
    return jnp.concatenate(taps + [jnp.zeros_like(cot)], axis=0)


def gram(ref, n, rows):
    total = None
    for r in range(rows // 8):
        block = halves(ref[:, 8 * r : 8 * r + 8, :].reshape(8 * n, STACK))
        part = dot3(block, block, NT)
        total = part if total is None else total + part
    sub = lax.broadcasted_iota(jnp.int32, total.shape, 0)
    lane = lax.broadcasted_iota(jnp.int32, total.shape, 1)
    kept = jnp.where(jnp.bitwise_and(sub, 7) == jnp.bitwise_and(lane, 7), total, 0.0)
    kept = jnp.sum(kept.reshape(n, 8, 8 * n), axis=1)
    source = lax.broadcasted_iota(jnp.int32, (8 * n, 128), 0)
    target = lax.broadcasted_iota(jnp.int32, (8 * n, 128), 1)
    fold = jnp.where(jnp.right_shift(source, 3) == target, 1.0, 0.0).astype(F32)
    return lax.dot_general(kept, fold, (NN, ((), ())), preferred_element_type=F32, precision=lax.Precision.HIGHEST)


def coefficients(table, n):
    rows = table.shape[0]
    sub = lax.broadcasted_iota(jnp.int32, table.shape, 0)
    lane = lax.broadcasted_iota(jnp.int32, table.shape, 1)
    diagonal = sub == lane
    result = jnp.ones((rows, 1), F32)
    b = 1
    while b < n:
        partner = jnp.bitwise_xor(sub, b) == lane
        own = jnp.where(diagonal, table, 0.0)
        cross = jnp.where(partner, table, 0.0)
        down = 1.0 - jnp.sum(cross, 1, keepdims=True) / (2.0 * (jnp.sum(own, 1, keepdims=True) + EPS))
        along = 1.0 - jnp.sum(cross, 0, keepdims=True) / (2.0 * (jnp.sum(own, 0, keepdims=True) + EPS))
        result = result * down
        if 2 * b < n:
            table = table * down * along
            moved = jnp.where(jnp.bitwise_and(sub, b) != 0, pltpu.roll(table, b, 0), pltpu.roll(table, rows - b, 0))
            table = table + moved
            moved = jnp.where(jnp.bitwise_and(lane, b) != 0, pltpu.roll(table, b, 1), pltpu.roll(table, 128 - b, 1))
            table = table + moved
        b *= 2
    return jnp.broadcast_to(result, (rows, 128))


def kernel(
    NY, NZ, NX,
    x_ref, cot_ref, w_hbm,
    out_ref, ig_ref, wg_ref,
    wv, wh, wl, ac, at, ct, ig, rp, rx, lt, cb, bt, yb, wf, ob, gm, gz, hm, hz, hy,
    wsem, za, cr, cl, acx, acp, atx, atp, rps, rxs, gms, gzs, ys, hms, hzs, hys, ps,
):
    NM = 2 * NX
    NDP = NY * NZ
    CD = x_ref.shape[1]
    CG = 8 * NM
    GROUPS = TAPS * NM // NY
    QUARTER = CG // NY
    dp = lax.axis_index("dp")
    me = lax.axis_index("mp")
    y, z = lax.div(dp, NZ), lax.rem(dp, NZ)
    x, c = lax.div(me, 2), lax.rem(me, 2)
    mate = me + 1 - 2 * c
    ring = lambda k: y * NZ + lax.rem(z + k + NZ, NZ)
    across = lambda k: 2 * lax.rem(x + k + NX, NX) + c

    def remote(src, dst, sems, k, r, to_dp, to_mp):
        return pltpu.make_async_remote_copy(
            src_ref=src, dst_ref=dst, send_sem=sems.at[0, k], recv_sem=sems.at[1, r],
            device_id=(to_dp, to_mp), device_id_type=MESH,
        )

    barrier = pltpu.get_barrier_semaphore()

    @pl.loop(1, NDP)
    def _(k):
        pl.semaphore_signal(barrier, inc=1, device_id=(lax.rem(dp + k, NDP), me), device_id_type=MESH)

    @pl.loop(1, NM)
    def _(k):
        pl.semaphore_signal(barrier, inc=1, device_id=(dp, lax.rem(me + k, NM)), device_id_type=MESH)

    weights_in = pltpu.make_async_copy(w_hbm, wv, wsem)
    weights_in.start()

    pre = x_ref[...]
    act = 0.5 * pre * (1.0 + lax.erf(pre * 0.7071067811865476))
    ac[me] = act.T
    at[me, z] = ac[me, pl.ds(pl.multiple_of(8 * z, 8), 8), :]
    cot = cot_ref[...]
    cot_t = jnp.concatenate([cot, jnp.zeros_like(cot)], axis=1).T[:64]
    ct[z] = cot_t

    weights_in.wait()
    for t in range(TAPS):
        high, low = halves(wv[:, t, :])
        wh[64 * t : 64 * t + 64, :] = high
        wl[64 * t : 64 * t + 64, :] = low
    wh[64 * TAPS :, :] = jnp.zeros_like(wh[64 * TAPS :, :])
    wl[64 * TAPS :, :] = jnp.zeros_like(wl[64 * TAPS :, :])

    stack_t = halves(stacked_taps(cot_t).T)
    for m in range(0, NM, 2):
        span = slice(CD * m, CD * m + 2 * CD)
        pair = dot3(stack_t, (wh[:, span], wl[:, span]), NN)
        ig[m] = pair[:, :CD]
        ig[m + 1] = pair[:, CD:]

    pl.semaphore_wait(barrier, NDP - 1 + NM - 1)

    def to_ring(k):
        there = lax.rem(z + k, NZ)
        rows = pl.ds(pl.multiple_of(8 * there, 8), 8)
        return remote(ac.at[me, rows], at.at[me, z], za, k, k, y * NZ + there, me)

    @pl.loop(1, NZ)
    def _(k):
        to_ring(k).start()

    def across_x(buf, sems, k):
        return remote(buf.at[me], buf.at[me], sems, k, k, dp, across(k))

    def to_mate(buf, sems, k):
        block = across(-k)
        return remote(buf.at[block], buf.at[block], sems, k, k, dp, mate)

    RIGHT, LEFT = NZ // 2, NZ // 2 - 1

    def rightward(s):
        image = lax.rem(z - s + 1 + NZ, NZ)
        return remote(ct.at[image], ct.at[image], cr, s, s, ring(1), me)

    def leftward(s):
        image = lax.rem(z + s - 1, NZ)
        return remote(ct.at[image], ct.at[image], cl, s, s, ring(-1), me)

    rightward(1).start()
    leftward(1).start()
    for k in range(1, NX):
        across_x(ac, acx, k).start()
    to_mate(ac, acp, 0).start()

    def mates_share(k):
        return remote(ig.at[2 * k + 1 - c], rp.at[k], rps, k, k, dp, mate)

    for k in range(NX):
        mates_share(k).start()

    def start_channels():
        @pl.loop(1, NZ)
        def _(k):
            to_ring(k).wait_recv()

        for k in range(1, NX):
            across_x(at, atx, k).start()
        to_mate(at, atp, 0).start()

    def pass_activations():
        for k in range(1, NX):
            across_x(ac, acx, k).wait_recv()
            to_mate(ac, acp, k).start()

    def share(k):
        own = across(k)
        return remote(ig.at[own], rx.at[x], rxs, k, k, dp, own)

    def start_shares():
        for k in range(NX):
            mates_share(k).wait_recv()
            ig[2 * k + c] = ig[2 * k + c] + rp[k]
        for k in range(1, NX):
            share(k).start()

    def pass_channels():
        for k in range(1, NX):
            across_x(at, atx, k).wait_recv()
            to_mate(at, atp, k).start()

    def channels_here():
        for k in range(NX):
            to_mate(at, atp, k).wait_recv()

    def leaf(image):
        stack = halves(stacked_taps(ct[image]))
        channels = halves(at[:, image].reshape(CG, PIX))
        lt[image] = dot3(channels, stack, NT) * (1.0 / PIX)

    def leaves_until(first, last):
        def work():
            @pl.loop(first, last)
            def _(j):
                half = lax.div(j + 1, 2)
                side = 1 - 2 * lax.rem(j, 2)
                leaf(lax.rem(z + side * half + NZ, NZ))
        return work

    items = [
        (1, pass_activations),
        (2, start_channels),
        (3, start_shares),
        (4, pass_channels),
        (5, channels_here),
        (5, leaves_until(0, min(7, NZ))),
    ]
    if NZ == 16:
        items += [(6, leaves_until(7, 11)), (7, leaves_until(11, 15)), (8, leaves_until(15, 16))]

    for s in range(1, RIGHT + 1):
        rightward(s).wait_recv()
        if s < RIGHT:
            rightward(s + 1).start()
        if s <= LEFT:
            leftward(s).wait_recv()
            if s < LEFT:
                leftward(s + 1).start()
        while items and (items[0][0] <= s or s == RIGHT):
            items.pop(0)[1]()

    def exchange(buf, n, mine, sems, device, between=None):
        there = lambda k: lax.rem(mine + k, n)

        @pl.loop(1, n)
        def _(k):
            remote(buf.at[mine], buf.at[mine], sems, k, k, *device(there(k))).start()

        if between is not None:
            between()

        @pl.loop(1, n)
        def _(k):
            remote(buf.at[mine], buf.at[there(n - k)], sems, k, k, *device(there(k))).wait_recv()

        total = buf[0]
        for k in range(1, n):
            total = total + buf[k]
        return total

    def sent(n, buf, mine, sems, device):
        there = lambda k: lax.rem(mine + k, n)

        @pl.loop(1, n)
        def _(k):
            remote(buf.at[mine], buf.at[mine], sems, k, k, *device(there(k))).wait_send()

    on_mp = lambda k: (dp, k)
    on_z = lambda k: (y * NZ + k, me)
    on_y = lambda k: (k * NZ + z, me)

    def convolve():
        for k in range(NX):
            to_mate(ac, acp, k).wait_recv()
        full = halves(ac[...].reshape(NM * CD, PIX))
        total = None
        for t in range(TAPS):
            rows = slice(64 * t, 64 * t + 64)
            product = dot3((wh[rows, :], wl[rows, :]), full, NN)
            moved = shifted(product, t // 3 - 1, t % 3 - 1)
            total = moved if total is None else total + moved
        out_ref[...] = total

    def finish_shares():
        total = ig[me]
        for k in range(1, NX):
            share(k).wait_recv()
            total = total + rx[lax.rem(x - k + NX, NX)]
        ig_ref[...] = total

    table = gram(lt, NZ, CG)
    lane = lax.broadcasted_iota(jnp.int32, (8, 128), 1)
    if NZ == 16:
        gm[me] = jnp.where(lane < 16, table[:8], pltpu.roll(table[8:], 16, 1))
    else:
        gm[me] = jnp.concatenate([table, jnp.zeros((8 - NZ, 128), F32)], axis=0)
    gz[z] = exchange(gm, NM, me, gms, on_mp)
    table = exchange(gz, NZ, z, gzs, on_z, convolve)
    if NZ == 16:
        table = jnp.concatenate([table, pltpu.roll(table, 112, 1)], axis=0)
    rows = table.shape[0]
    cb[0:rows, :] = coefficients(table, NZ)
    total = None
    for i in range(NZ):
        scale = jnp.concatenate([cb[i : i + 1, :]] * (STACK // 128), axis=1)
        term = lt[i] * scale
        total = term if total is None else total + term
    bt[...] = total
    yb[y] = bt[pl.ds(pl.multiple_of(QUARTER * y, 8), QUARTER), :]

    def to_y(k):
        there = lax.rem(y + k, NY)
        rows = pl.ds(pl.multiple_of(QUARTER * there, 8), QUARTER)
        return remote(bt.at[rows], yb.at[y], ys, k, k, there * NZ + z, me)

    for k in range(1, NY):
        to_y(k).start()
    finish_shares()
    for k in range(1, NY):
        to_y(k).wait_recv()
    table = gram(yb, NY, QUARTER)
    hm[me] = jnp.concatenate([table, jnp.zeros((8 - NY, 128), F32)], axis=0)
    hy[y] = exchange(hm, NM, me, hms, on_mp)
    hz[z] = exchange(hy, NY, y, hys, on_y)
    table = exchange(hz, NZ, z, hzs, on_z)
    cb[0:8, :] = coefficients(table, NY)
    total = None
    for i in range(NY):
        scale = jnp.concatenate([cb[i : i + 1, :]] * (STACK // 128), axis=1)
        term = yb[i] * scale
        total = term if total is None else total + term
    wf[...] = total

    def group(j):
        m, tap = divmod(j, TAPS)
        number = NZ * NM * tap + NZ * ((QUARTER // 8) * y + m) + z
        owner, slot = lax.div(number, GROUPS), lax.rem(number, GROUPS)
        source = wf.at[pl.ds(8 * m, 8), pl.ds(128 * (tap // 2), 128)]
        return owner, slot, source

    for j in range(GROUPS):
        owner, slot, source = group(j)

        @pl.when(owner != dp)
        def _():
            remote(source, ob.at[slot], ps, j, slot, owner, me).start()

        @pl.when(owner == dp)
        def _():
            pltpu.make_async_copy(source, ob.at[slot], ps.at[1, slot]).start()

    for s in range(GROUPS):
        pltpu.make_async_copy(ob.at[s], ob.at[s], ps.at[1, s]).wait()
        tap = lax.div(GROUPS * dp + s, NZ * NM)
        piece = ob[s]
        wg_ref[8 * s : 8 * s + 8, :] = jnp.where(lax.rem(tap, 2) == 1, pltpu.roll(piece, 64, 1), piece)

    @pl.loop(1, NZ)
    def _(k):
        to_ring(k).wait_send()

    for s in range(1, RIGHT + 1):
        rightward(s).wait_send()
    for s in range(1, LEFT + 1):
        leftward(s).wait_send()
    for k in range(NX):
        if k:
            across_x(ac, acx, k).wait_send()
            across_x(at, atx, k).wait_send()
            share(k).wait_send()
        to_mate(ac, acp, k).wait_send()
        to_mate(at, atp, k).wait_send()
        mates_share(k).wait_send()
    for k in range(1, NY):
        to_y(k).wait_send()
    sent(NM, gm, me, gms, on_mp)
    sent(NZ, gz, z, gzs, on_z)
    sent(NM, hm, me, hms, on_mp)
    sent(NZ, hz, z, hzs, on_z)
    sent(NY, hy, y, hys, on_y)
    for j in range(GROUPS):
        owner, slot, source = group(j)

        @pl.when(owner != dp)
        def _():
            remote(source, ob.at[slot], ps, j, slot, owner, me).wait_send()


def gelu_slope(values):
    return (
        0.5 * (1.0 + lax.erf(values * 0.7071067811865476))
        + values * jnp.exp(-0.5 * values * values) * 0.3989422804014327
    )


def local(NY, NZ, NX, preact, weights, cotangent):
    NM = 2 * NX
    CD = preact.shape[3]
    CG = 8 * NM
    QUARTER = CG // NY
    GROUPS = TAPS * NM // NY
    vmem = lambda *shape: pltpu.VMEM(shape, F32)
    sems = lambda n: pltpu.SemaphoreType.DMA((2, n))
    whole = pl.BlockSpec(memory_space=pltpu.VMEM)
    pre = preact.reshape(PIX, CD)
    out, ig, wg = pl.pallas_call(
        functools.partial(kernel, NY, NZ, NX),
        out_shape=(
            jax.ShapeDtypeStruct((64, PIX), F32),
            jax.ShapeDtypeStruct((PIX, CD), F32),
            jax.ShapeDtypeStruct((8 * GROUPS, 128), F32),
        ),
        in_specs=[whole, whole, pl.BlockSpec(memory_space=pl.ANY)],
        out_specs=(whole, whole, whole),
        scratch_shapes=[
            vmem(*weights.shape),
            pltpu.VMEM((STACK, NM * CD), BF16),
            pltpu.VMEM((STACK, NM * CD), BF16),
            vmem(NM, CD, PIX),
            vmem(NM, NZ, 8, PIX),
            vmem(NZ, 64, PIX),
            vmem(NM, PIX, CD),
            vmem(NX, PIX, CD),
            vmem(NX, PIX, CD),
            vmem(NZ, CG, STACK),
            vmem(16, 128),
            vmem(CG, STACK),
            vmem(NY, QUARTER, STACK),
            vmem(QUARTER, STACK),
            vmem(GROUPS, 8, 128),
            vmem(NM, 8, 128),
            vmem(NZ, 8, 128),
            vmem(NM, 8, 128),
            vmem(NZ, 8, 128),
            vmem(NY, 8, 128),
            pltpu.SemaphoreType.DMA,
            sems(NZ), sems(NZ), sems(NZ),
            sems(NX), sems(NX), sems(NX), sems(NX), sems(NX), sems(NX),
            sems(NM), sems(NZ), sems(NY), sems(NM), sems(NZ), sems(NY),
            sems(GROUPS),
        ],
        compiler_params=pltpu.CompilerParams(collective_id=0, has_side_effects=True),
        name="step",
    )(pre, cotangent.reshape(PIX, 64), weights)
    output = out.T.reshape(1, SIDE, SIDE, 64)
    input_grad = (ig * gelu_slope(pre)).reshape(preact.shape)
    return output, input_grad, wg[:, :64].T


def build(mesh, NY, NZ, NX):
    placed = (P("dp", None, None, "mp"), P("mp", None, None), P("dp", None, None, "mp"))
    return jax.shard_map(
        functools.partial(local, NY, NZ, NX),
        mesh=mesh,
        in_specs=placed,
        out_specs=(P("dp", None, None, "mp"), P("dp", None, None, "mp"), P("mp", "dp")),
        check_vma=False,
    )


def solution(mesh):
    return build(mesh, 4, mesh.shape["dp"] // 4, mesh.shape["mp"] // 2)
```

```python
import functools

import jax
import jax.numpy as jnp
from jax import lax
from jax.experimental import pallas as pl
from jax.experimental.pallas import tpu as pltpu
from jax.sharding import PartitionSpec as P

MESH = pl.DeviceIdType.MESH
F32 = jnp.float32
BF16 = jnp.bfloat16
EPS = 1e-06
SIDE = 16
PIX = SIDE * SIDE
TAPS = 9
STACK = 640


def halves(values):
    high = values.astype(BF16)
    low = (values - high.astype(F32)).astype(BF16)
    return high, low


def dot3(a, b, dims):
    one = lambda p, q: lax.dot_general(p, q, (dims, ((), ())), preferred_element_type=F32)
    return one(a[0], b[0]) + (one(a[0], b[1]) + one(a[1], b[0]))


NN = ((1,), (0,))
NT = ((1,), (1,))


def shifted(values, dy, dx):
    pixel = lax.broadcasted_iota(jnp.int32, values.shape, 1)
    column = jnp.bitwise_and(pixel, SIDE - 1)
    inside = None
    if dx:
        inside = (column >= 1) if dx < 0 else (column < SIDE - 1)
    if dy:
        rows = (pixel >= SIDE) if dy < 0 else (pixel < PIX - SIDE)
        inside = rows if inside is None else jnp.logical_and(inside, rows)
    step = SIDE * dy + dx
    if step == 0:
        return values
    return jnp.where(inside, pltpu.roll(values, (-step) % PIX, 1), 0.0)


def stacked_taps(cot):
    taps = [shifted(cot, 1 - t // 3, 1 - t % 3) for t in range(TAPS)]
    return jnp.concatenate(taps + [jnp.zeros_like(cot)], axis=0)


def gram(ref, n, rows):
    total = None
    for r in range(rows // 8):
        block = halves(ref[:, 8 * r : 8 * r + 8, :].reshape(8 * n, STACK))
        part = dot3(block, block, NT)
        total = part if total is None else total + part
    sub = lax.broadcasted_iota(jnp.int32, total.shape, 0)
    lane = lax.broadcasted_iota(jnp.int32, total.shape, 1)
    kept = jnp.where(jnp.bitwise_and(sub, 7) == jnp.bitwise_and(lane, 7), total, 0.0)
    kept = jnp.sum(kept.reshape(n, 8, 8 * n), axis=1)
    source = lax.broadcasted_iota(jnp.int32, (8 * n, 128), 0)
    target = lax.broadcasted_iota(jnp.int32, (8 * n, 128), 1)
    fold = jnp.where(jnp.right_shift(source, 3) == target, 1.0, 0.0).astype(F32)
    return lax.dot_general(kept, fold, (NN, ((), ())), preferred_element_type=F32, precision=lax.Precision.HIGHEST)


def packed(table, n):
    per = min(n, 128 // n)
    rows = []
    for r in range(n // per):
        row = table[r * per : r * per + 1]
        for i in range(1, per):
            row = row + pltpu.roll(table[r * per + i : r * per + i + 1], n * i, 1)
        rows.append(row)
    return rows[0] if len(rows) == 1 else jnp.concatenate(rows, axis=0)


def unpacked(rows, n, scratch):
    per = min(n, 128 // n)
    held = max(n, 8)
    if n < 8:
        scratch[0:8, :] = jnp.zeros((8, 128), F32)
    for i in range(n):
        row = rows[i // per : i // per + 1]
        scratch[i : i + 1, :] = pltpu.roll(row, (128 - n * (i % per)) % 128, 1) if i % per else row
    return scratch[0:held, :]


def coefficients(table, n):
    rows = table.shape[0]
    sub = lax.broadcasted_iota(jnp.int32, table.shape, 0)
    lane = lax.broadcasted_iota(jnp.int32, table.shape, 1)
    diagonal = sub == lane
    result = jnp.ones((rows, 1), F32)
    b = 1
    while b < n:
        partner = jnp.bitwise_xor(sub, b) == lane
        own = jnp.where(diagonal, table, 0.0)
        cross = jnp.where(partner, table, 0.0)
        down = 1.0 - jnp.sum(cross, 1, keepdims=True) / (2.0 * (jnp.sum(own, 1, keepdims=True) + EPS))
        along = 1.0 - jnp.sum(cross, 0, keepdims=True) / (2.0 * (jnp.sum(own, 0, keepdims=True) + EPS))
        result = result * down
        if 2 * b < n:
            table = table * down * along
            moved = jnp.where(jnp.bitwise_and(sub, b) != 0, pltpu.roll(table, b, 0), pltpu.roll(table, rows - b, 0))
            table = table + moved
            moved = jnp.where(jnp.bitwise_and(lane, b) != 0, pltpu.roll(table, b, 1), pltpu.roll(table, 128 - b, 1))
            table = table + moved
        b *= 2
    return jnp.broadcast_to(result, (rows, 128))


def gelu_slope(values):
    return (
        0.5 * (1.0 + lax.erf(values * 0.7071067811865476))
        + values * jnp.exp(-0.5 * values * values) * 0.3989422804014327
    )


CHUNKS = 2


def kernel(
    NY, NZ, NX,
    x_ref, cot_ref, w_hbm,
    out_ref, ig_ref, wg_ref,
    wv, wh, wl, ac, at, ct, ig, rp, rx, lt, cb, bt, yb, pk, ob, gm, gz, hm, hz,
    wsem, za, cr, cl, acx, acp, atx, atp, rps, rxs, gms, gzs, ys, hms, hzs, ps,
):
    NM = 2 * NX
    CD = x_ref.shape[1]
    CG = 8 * NM
    GROUPS = TAPS * NM // NY
    QUARTER = CG // NY
    HALF = NZ // 2
    dp = lax.axis_index("dp")
    me = lax.axis_index("mp")
    y, z = lax.div(dp, NZ), lax.rem(dp, NZ)
    x, c = lax.div(me, 2), lax.rem(me, 2)
    mate = me + 1 - 2 * c
    ring = lambda k: y * NZ + lax.rem(z + k + NZ, NZ)
    across = lambda k: 2 * lax.rem(x + k + NX, NX) + c

    def remote(src, dst, sems, k, r, to_dp, to_mp):
        return pltpu.make_async_remote_copy(
            src_ref=src, dst_ref=dst, send_sem=sems.at[0, k], recv_sem=sems.at[1, r],
            device_id=(to_dp, to_mp), device_id_type=MESH,
        )

    with jax.named_scope("signals"):
        barrier = pltpu.get_barrier_semaphore()

        @pl.loop(1, NZ)
        def _(k):
            pl.semaphore_signal(barrier, inc=1, device_id=(ring(k), me), device_id_type=MESH)

        for k in range(1, NY):
            pl.semaphore_signal(barrier, inc=1, device_id=(lax.rem(y + k, NY) * NZ + z, me), device_id_type=MESH)
        for k in range(1, NM):
            pl.semaphore_signal(barrier, inc=1, device_id=(dp, lax.rem(me + k, NM)), device_id_type=MESH)

    weights_in = pltpu.make_async_copy(w_hbm, wv, wsem)
    weights_in.start()

    with jax.named_scope("gelu"):
        pre = x_ref[...]
        act = 0.5 * pre * (1.0 + lax.erf(pre * 0.7071067811865476))
        ac[me] = act.T
        at[me, 0] = ac[me, pl.ds(pl.multiple_of(8 * z, 8), 8), :]
        cot = cot_ref[...]
        cot_t = jnp.concatenate([cot, jnp.zeros_like(cot)], axis=1).T[:64]
        ct[z] = cot_t

    with jax.named_scope("wprep"):
        weights_in.wait()
        for t in range(TAPS):
            high, low = halves(wv[t])
            wh[64 * t : 64 * t + 64, :] = high
            wl[64 * t : 64 * t + 64, :] = low
        wh[64 * TAPS :, :] = jnp.zeros_like(wh[64 * TAPS :, :])
        wl[64 * TAPS :, :] = jnp.zeros_like(wl[64 * TAPS :, :])

    with jax.named_scope("igpart"):
        stack_t = halves(stacked_taps(cot_t).T)
        for m in range(0, NM, 2):
            span = slice(CD * m, CD * m + 2 * CD)
            pair = dot3(stack_t, (wh[:, span], wl[:, span]), NN)
            ig[m] = pair[:, :CD]
            ig[m + 1] = pair[:, CD:]

    with jax.named_scope("barwait"):
        pl.semaphore_wait(barrier, NZ - 1 + NY - 1 + NM - 1)

    def offset(j):
        half = lax.div(j + 1, 2)
        return half * (2 * lax.rem(j, 2) - 1)

    def to_ring(j):
        there = lax.rem(z + offset(j) + NZ, NZ)
        rows = pl.ds(pl.multiple_of(8 * there, 8), 8)
        return remote(ac.at[me, rows], at.at[me, j], za, j, j, y * NZ + there, me)

    def across_x(k):
        return remote(ac.at[me], ac.at[me], acx, k, k, dp, across(k))

    def to_mate(k):
        block = across(-k)
        return remote(ac.at[block], ac.at[block], acp, k, k, dp, mate)

    def part_across_x(p, k):
        part = at.at[me, pl.ds(HALF * p, HALF)]
        return remote(part, part, atx, NX * p + k, NX * p + k, dp, across(k))

    def part_to_mate(p, k):
        part = at.at[across(-k), pl.ds(HALF * p, HALF)]
        return remote(part, part, atp, NX * p + k, NX * p + k, dp, mate)

    RIGHT, LEFT = NZ // 2, NZ // 2 - 1
    TALL = 64 // CHUNKS

    def rightward(s, q):
        part = ct.at[lax.rem(z - s + 1 + NZ, NZ), pl.ds(TALL * q, TALL)]
        return remote(part, part, cr, CHUNKS * s + q, CHUNKS * s + q, ring(1), me)

    def leftward(s, q):
        part = ct.at[lax.rem(z + s - 1, NZ), pl.ds(TALL * q, TALL)]
        return remote(part, part, cl, CHUNKS * s + q, CHUNKS * s + q, ring(-1), me)

    for q in range(CHUNKS):
        rightward(1, q).start()
        leftward(1, q).start()

    @pl.loop(1, NZ)
    def _(j):
        to_ring(j).start()

    def mates_share(k):
        return remote(ig.at[2 * k + 1 - c], rp.at[k], rps, k, k, dp, mate)

    for k in range(NX):
        mates_share(k).start()

    def start_part(p):
        @pl.loop(max(1, HALF * p), HALF * (p + 1))
        def _(j):
            to_ring(j).wait_recv()

        for k in range(1, NX):
            part_across_x(p, k).start()
        part_to_mate(p, 0).start()

    def pass_part(p):
        for k in range(1, NX):
            part_across_x(p, k).wait_recv()
            part_to_mate(p, k).start()

    def part_here(p):
        for k in range(NX):
            part_to_mate(p, k).wait_recv()

    def start_activations():
        for k in range(1, NX):
            across_x(k).start()
        to_mate(0).start()

    def pass_activations():
        for k in range(1, NX):
            across_x(k).wait_recv()
            to_mate(k).start()

    def share(k):
        own = across(k)
        return remote(ig.at[own], rx.at[x], rxs, k, k, dp, own)

    def add_shares():
        for k in range(NX):
            mates_share(k).wait_recv()
            ig[2 * k + c] = ig[2 * k + c] + rp[k]

    def start_shares():
        for k in range(1, NX):
            share(k).start()

    def leaves(first, last):
        @pl.loop(first, last)
        def _(j):
            image = lax.rem(z - offset(j) + NZ, NZ)
            stack = halves(stacked_taps(ct[image]))
            channels = halves(at[:, j].reshape(CG, PIX))
            lt[image] = dot3(channels, stack, NT) * (1.0 / PIX)

    if NZ == 16:
        plan = {
            (2, 0): [(start_part, 0)],
            (3, 0): [(add_shares,)],
            (4, 0): [(start_part, 1), (start_activations,), (start_shares,)],
            (5, 0): [(pass_part, 0)],
            (6, 0): [(part_here, 0), (leaves, 0, 4)],
            (6, 1): [(leaves, 4, 8)],
            (7, 1): [(pass_part, 1)],
            (8, 1): [(part_here, 1), (leaves, 8, 16)],
        }
    else:
        plan = {
            (RIGHT, 1): [
                (start_part, 0), (add_shares,), (start_part, 1), (start_activations,), (start_shares,),
                (pass_part, 0), (part_here, 0), (pass_part, 1), (part_here, 1), (leaves, 0, NZ),
            ],
        }

    for s in range(1, RIGHT + 1):
        for q in range(CHUNKS):
            with jax.named_scope(f"wait{s}_{q}"):
                rightward(s, q).wait_recv()
                if s < RIGHT:
                    rightward(s + 1, q).start()
                if s <= LEFT:
                    leftward(s, q).wait_recv()
                    if s < LEFT:
                        leftward(s + 1, q).start()
            for work in plan.get((s, q), []):
                with jax.named_scope(f"{work[0].__name__}{work[1] if len(work) > 1 else 0}"):
                    work[0](*work[1:])

    def exchange(buf, n, mine, sems, device, between=None):
        there = lambda k: lax.rem(mine + k, n)

        @pl.loop(1, n)
        def _(k):
            remote(buf.at[mine], buf.at[mine], sems, k, k, *device(there(k))).start()

        if between is not None:
            between()

        @pl.loop(1, n)
        def _(k):
            remote(buf.at[mine], buf.at[there(n - k)], sems, k, k, *device(there(k))).wait_recv()

        total = buf[0]
        for k in range(1, n):
            total = total + buf[k]
        return total

    def sent(n, buf, mine, sems, device):
        there = lambda k: lax.rem(mine + k, n)

        @pl.loop(1, n)
        def _(k):
            remote(buf.at[mine], buf.at[mine], sems, k, k, *device(there(k))).wait_send()

    on_mp = lambda k: (dp, k)
    on_z = lambda k: (y * NZ + k, me)
    on_y_mp = lambda k: (lax.div(k, NM) * NZ + z, lax.rem(k, NM))

    def convolve():
        for k in range(NX):
            to_mate(k).wait_recv()
        full = halves(ac[...].reshape(NM * CD, PIX))
        total = None
        for t in range(TAPS):
            rows = slice(64 * t, 64 * t + 64)
            product = dot3((wh[rows, :], wl[rows, :]), full, NN)
            moved = shifted(product, t // 3 - 1, t % 3 - 1)
            total = moved if total is None else total + moved
        total = jnp.concatenate([total, jnp.zeros_like(total)], axis=0).T
        out_ref[...] = total[:, :64]

    def finish_shares():
        total = ig[me]
        for k in range(1, NX):
            share(k).wait_recv()
            total = total + rx[lax.rem(x - k + NX, NX)]
        ig_ref[...] = total * gelu_slope(x_ref[...])

    with jax.named_scope("gram16"):
        gm[me] = packed(gram(lt, NZ, CG), NZ)
    with jax.named_scope("g16mp"):
        gz[z] = exchange(gm, NM, me, gms, on_mp, pass_activations)
    with jax.named_scope("g16z"):
        table = exchange(gz, NZ, z, gzs, on_z, convolve)
    with jax.named_scope("coef16"):
        table = unpacked(table, NZ, cb)
        rows = table.shape[0]
        cb[0:rows, :] = coefficients(table, NZ)
    with jax.named_scope("comb16"):
        total = None
        for i in range(NZ):
            scale = jnp.concatenate([cb[i : i + 1, :]] * (STACK // 128), axis=1)
            term = lt[i] * scale
            total = term if total is None else total + term
        bt[...] = total
        yb[y] = bt[pl.ds(pl.multiple_of(QUARTER * y, 8), QUARTER), :]

    def to_y(k):
        there = lax.rem(y + k, NY)
        rows = pl.ds(pl.multiple_of(QUARTER * there, 8), QUARTER)
        return remote(bt.at[rows], yb.at[y], ys, k, k, there * NZ + z, me)

    with jax.named_scope("ywait"):
        for k in range(1, NY):
            to_y(k).start()
        for k in range(1, NY):
            to_y(k).wait_recv()

    def group(j):
        m, tap = divmod(j, TAPS)
        number = NZ * NM * tap + NZ * ((QUARTER // 8) * y + m) + z
        return lax.div(number, GROUPS), lax.rem(number, GROUPS)

    lower = lax.broadcasted_iota(jnp.int32, (8, 128), 1) < 64

    def send_groups():
        with jax.named_scope("permsend"):
            for j in range(GROUPS):
                m, tap = divmod(j, TAPS)
                span = slice(128 * (tap // 2), 128 * (tap // 2) + 128)
                for h in range(NY // 2):
                    left = yb[2 * h, 8 * m : 8 * m + 8, span]
                    right = yb[2 * h + 1, 8 * m : 8 * m + 8, span]
                    if tap % 2:
                        left = pltpu.roll(left, 64, 1)
                    else:
                        right = pltpu.roll(right, 64, 1)
                    pk[j, 8 * h : 8 * h + 8, :] = jnp.where(lower, left, right)
            for j in range(GROUPS):
                owner, slot = group(j)

                @pl.when(owner != dp)
                def _():
                    remote(pk.at[j], ob.at[slot], ps, j, slot, owner, me).start()

                @pl.when(owner == dp)
                def _():
                    pltpu.make_async_copy(pk.at[j], ob.at[slot], ps.at[1, slot]).start()

    def settle():
        finish_shares()

        @pl.loop(1, NZ)
        def _(j):
            to_ring(j).wait_send()

        for q in range(CHUNKS):
            for s in range(1, RIGHT + 1):
                rightward(s, q).wait_send()
            for s in range(1, LEFT + 1):
                leftward(s, q).wait_send()
        for k in range(NX):
            if k:
                across_x(k).wait_send()
                share(k).wait_send()
                for p in range(2):
                    part_across_x(p, k).wait_send()
            to_mate(k).wait_send()
            mates_share(k).wait_send()
            for p in range(2):
                part_to_mate(p, k).wait_send()
        for k in range(1, NY):
            to_y(k).wait_send()
        sent(NM, gm, me, gms, on_mp)
        sent(NZ, gz, z, gzs, on_z)

    with jax.named_scope("gram4"):
        here = NM * y + me
        hm[here] = packed(gram(yb, NY, QUARTER), NY)
    with jax.named_scope("g4ymp"):
        hz[z] = exchange(hm, NY * NM, here, hms, on_y_mp, send_groups)
    with jax.named_scope("g4z"):
        table = exchange(hz, NZ, z, hzs, on_z, settle)
    with jax.named_scope("coef4"):
        table = unpacked(table, NY, cb)
        cb[0:8, :] = coefficients(table, NY)
        scales = [jnp.where(lower, cb[2 * h : 2 * h + 1, :], cb[2 * h + 1 : 2 * h + 2, :]) for h in range(NY // 2)]
    with jax.named_scope("permrecv"):
        pieces = []
        for s in range(GROUPS):
            pltpu.make_async_copy(ob.at[s], ob.at[s], ps.at[1, s]).wait()
            piece = None
            for h in range(NY // 2):
                term = ob[s, 8 * h : 8 * h + 8, :] * scales[h]
                piece = term if piece is None else piece + term
            pieces.append(piece)
        columns = jnp.concatenate(pieces, axis=0)
        columns = columns + pltpu.roll(columns, 64, 1)
        fill = -8 * GROUPS % 128
        columns = jnp.concatenate([columns, jnp.zeros((fill, 128), F32)], axis=0).T
        wg_ref[...] = columns[:64, : 8 * GROUPS]

    with jax.named_scope("drain"):
        sent(NY * NM, hm, here, hms, on_y_mp)
        sent(NZ, hz, z, hzs, on_z)
        for j in range(GROUPS):
            owner, slot = group(j)

            @pl.when(owner != dp)
            def _():
                remote(pk.at[j], ob.at[slot], ps, j, slot, owner, me).wait_send()


def local(NY, NZ, NX, preact, weights, cotangent):
    NM = 2 * NX
    CD = preact.shape[3]
    CG = 8 * NM
    QUARTER = CG // NY
    GROUPS = TAPS * NM // NY
    rows16 = NZ // min(NZ, 128 // NZ)
    vmem = lambda *shape: pltpu.VMEM(shape, F32)
    sems = lambda n: pltpu.SemaphoreType.DMA((2, n))
    whole = pl.BlockSpec(memory_space=pltpu.VMEM)
    output, input_grad, weight_grad = pl.pallas_call(
        functools.partial(kernel, NY, NZ, NX),
        out_shape=(
            jax.ShapeDtypeStruct((PIX, 64), F32),
            jax.ShapeDtypeStruct((PIX, CD), F32),
            jax.ShapeDtypeStruct((64, 8 * GROUPS), F32),
        ),
        in_specs=[whole, whole, pl.BlockSpec(memory_space=pl.ANY)],
        out_specs=(whole, whole, whole),
        scratch_shapes=[
            vmem(TAPS, 64, NM * CD),
            pltpu.VMEM((STACK, NM * CD), BF16),
            pltpu.VMEM((STACK, NM * CD), BF16),
            vmem(NM, CD, PIX),
            vmem(NM, NZ, 8, PIX),
            vmem(NZ, 64, PIX),
            vmem(NM, PIX, CD),
            vmem(NX, PIX, CD),
            vmem(NX, PIX, CD),
            vmem(NZ, CG, STACK),
            vmem(16, 128),
            vmem(CG, STACK),
            vmem(NY, QUARTER, STACK),
            vmem(GROUPS, 4 * NY, 128),
            vmem(GROUPS, 4 * NY, 128),
            vmem(NM, rows16, 128),
            vmem(NZ, rows16, 128),
            vmem(NY * NM, 1, 128),
            vmem(NZ, 1, 128),
            pltpu.SemaphoreType.DMA,
            sems(NZ), sems(CHUNKS * NZ), sems(CHUNKS * NZ),
            sems(NX), sems(NX), sems(2 * NX), sems(2 * NX), sems(NX), sems(NX),
            sems(NM), sems(NZ), sems(NY), sems(NY * NM), sems(NZ),
            sems(GROUPS),
        ],
        compiler_params=pltpu.CompilerParams(collective_id=0, has_side_effects=True),
        name="step",
    )(preact.reshape(PIX, CD), cotangent.reshape(PIX, 64), weights.transpose(1, 0, 2))
    return output.reshape(1, SIDE, SIDE, 64), input_grad.reshape(preact.shape), weight_grad


def build(mesh, NY, NZ, NX):
    placed = (P("dp", None, None, "mp"), P("mp", None, None), P("dp", None, None, "mp"))
    return jax.shard_map(
        functools.partial(local, NY, NZ, NX),
        mesh=mesh,
        in_specs=placed,
        out_specs=(P("dp", None, None, "mp"), P("dp", None, None, "mp"), P("mp", "dp")),
        check_vma=False,
    )


def solution(mesh):
    return build(mesh, 4, mesh.shape["dp"] // 4, mesh.shape["mp"] // 2)
```

```python
import functools

import jax
import jax.numpy as jnp
from jax import lax
from jax.experimental import pallas as pl
from jax.experimental.pallas import tpu as pltpu
from jax.sharding import PartitionSpec as P

MESH = pl.DeviceIdType.MESH
F32 = jnp.float32
BF16 = jnp.bfloat16
EPS = 1e-06
SIDE = 16
PIX = SIDE * SIDE
TAPS = 9
STACK = 640


def halves(values):
    high = values.astype(BF16)
    low = (values - high.astype(F32)).astype(BF16)
    return high, low


def dot3(a, b, dims):
    one = lambda p, q: lax.dot_general(p, q, (dims, ((), ())), preferred_element_type=F32)
    return one(a[0], b[0]) + (one(a[0], b[1]) + one(a[1], b[0]))


def dot3_joined(a, b, dims):
    one = lambda p, q: lax.dot_general(p, q, (dims, ((), ())), preferred_element_type=F32)
    rows = a[0].shape[0]
    both = one(jnp.concatenate(a, axis=0), b[0])
    return both[:rows] + (both[rows:] + one(a[0], b[1]))


NN = ((1,), (0,))
NT = ((1,), (1,))


def shifted(values, dy, dx):
    pixel = lax.broadcasted_iota(jnp.int32, values.shape, 1)
    column = jnp.bitwise_and(pixel, SIDE - 1)
    inside = None
    if dx:
        inside = (column >= 1) if dx < 0 else (column < SIDE - 1)
    if dy:
        rows = (pixel >= SIDE) if dy < 0 else (pixel < PIX - SIDE)
        inside = rows if inside is None else jnp.logical_and(inside, rows)
    step = SIDE * dy + dx
    if step == 0:
        return values
    return jnp.where(inside, pltpu.roll(values, (-step) % PIX, 1), 0.0)


def stacked_taps(cot):
    taps = [shifted(cot, 1 - t // 3, 1 - t % 3) for t in range(TAPS)]
    return jnp.concatenate(taps + [jnp.zeros_like(cot)], axis=0)


def folded(total, n, bits):
    size = 1 << bits
    sub = lax.broadcasted_iota(jnp.int32, total.shape, 0)
    lane = lax.broadcasted_iota(jnp.int32, total.shape, 1)
    kept = jnp.where(jnp.bitwise_and(sub, size - 1) == jnp.bitwise_and(lane, size - 1), total, 0.0)
    kept = jnp.sum(kept.reshape(n, size, size * n), axis=1)
    source = lax.broadcasted_iota(jnp.int32, (size * n, 128), 0)
    target = lax.broadcasted_iota(jnp.int32, (size * n, 128), 1)
    fold = jnp.where(jnp.right_shift(source, bits) == target, 1.0, 0.0).astype(F32)
    return lax.dot_general(kept, fold, (NN, ((), ())), preferred_element_type=F32, precision=lax.Precision.HIGHEST)


def gram(ref, n, rows):
    total = None
    for r in range(rows // 8):
        block = halves(ref[:, 8 * r : 8 * r + 8, :].reshape(8 * n, STACK))
        both = jnp.concatenate(block, axis=0)
        part = lax.dot_general(both, block[0], (NT, ((), ())), preferred_element_type=F32)
        total = part if total is None else total + part
    low = total[8 * n :]
    return folded(total[: 8 * n] + (low + low.T), n, 3)


def packed(table, n):
    per = min(n, 128 // n)
    rows = []
    for r in range(n // per):
        row = table[r * per : r * per + 1]
        for i in range(1, per):
            row = row + pltpu.roll(table[r * per + i : r * per + i + 1], n * i, 1)
        rows.append(row)
    return rows[0] if len(rows) == 1 else jnp.concatenate(rows, axis=0)


def unpacked(rows, n, scratch):
    per = min(n, 128 // n)
    held = max(n, 8)
    if n < 8:
        scratch[0:8, :] = jnp.zeros((8, 128), F32)
    for i in range(n):
        row = rows[i // per : i // per + 1]
        scratch[i : i + 1, :] = pltpu.roll(row, (128 - n * (i % per)) % 128, 1) if i % per else row
    return scratch[0:held, :]


def coefficients(table, n):
    rows = table.shape[0]
    sub = lax.broadcasted_iota(jnp.int32, table.shape, 0)
    lane = lax.broadcasted_iota(jnp.int32, table.shape, 1)
    diagonal = sub == lane
    result = jnp.ones((rows, 1), F32)
    b = 1
    while b < n:
        partner = jnp.bitwise_xor(sub, b) == lane
        own = jnp.where(diagonal, table, 0.0)
        cross = jnp.where(partner, table, 0.0)
        down = 1.0 - jnp.sum(cross, 1, keepdims=True) / (2.0 * (jnp.sum(own, 1, keepdims=True) + EPS))
        along = 1.0 - jnp.sum(cross, 0, keepdims=True) / (2.0 * (jnp.sum(own, 0, keepdims=True) + EPS))
        result = result * down
        if 2 * b < n:
            table = table * down * along
            moved = jnp.where(jnp.bitwise_and(sub, b) != 0, pltpu.roll(table, b, 0), pltpu.roll(table, rows - b, 0))
            table = table + moved
            moved = jnp.where(jnp.bitwise_and(lane, b) != 0, pltpu.roll(table, b, 1), pltpu.roll(table, 128 - b, 1))
            table = table + moved
        b *= 2
    return jnp.broadcast_to(result, (rows, 128))


def gelu_slope(values):
    return (
        0.5 * (1.0 + lax.erf(values * 0.7071067811865476))
        + values * jnp.exp(-0.5 * values * values) * 0.3989422804014327
    )


CHUNKS = 4


def kernel(
    NY, NZ, NX,
    x_hbm, cot_hbm, w_hbm,
    out_hbm, ig_hbm, wg_hbm,
    x_ref, cot_ref, out_ref, ig_ref, wg_ref, wv, wh, wl, ac, at, ct, ig, rp, rx, sh, sl, lt, cb, bt, yb, pk, ob, gm, gz, hm, hz,
    isem, osem, za, cr, cl, acx, acp, atx, atp, rps, rxs, gms, gzs, ys, hms, hzs, ps,
):
    NM = 2 * NX
    CD = x_ref.shape[1]
    CG = 8 * NM
    GROUPS = TAPS * NM // NY
    QUARTER = CG // NY
    HALF = NZ // 2
    dp = lax.axis_index("dp")
    me = lax.axis_index("mp")
    y, z = lax.div(dp, NZ), lax.rem(dp, NZ)
    x, c = lax.div(me, 2), lax.rem(me, 2)
    mate = me + 1 - 2 * c
    ring = lambda k: y * NZ + lax.rem(z + k + NZ, NZ)
    across = lambda k: 2 * lax.rem(x + k + NX, NX) + c

    def remote(src, dst, sems, k, r, to_dp, to_mp):
        return pltpu.make_async_remote_copy(
            src_ref=src, dst_ref=dst, send_sem=sems.at[0, k], recv_sem=sems.at[1, r],
            device_id=(to_dp, to_mp), device_id_type=MESH,
        )

    x_in = pltpu.make_async_copy(x_hbm, x_ref, isem.at[0])
    cot_in = pltpu.make_async_copy(cot_hbm, cot_ref, isem.at[1])
    weights_in = pltpu.make_async_copy(w_hbm, wv, isem.at[2])
    x_in.start()
    cot_in.start()

    with jax.named_scope("signals"):
        barrier = pltpu.get_barrier_semaphore()

        @pl.loop(1, NZ)
        def _(k):
            pl.semaphore_signal(barrier, inc=1, device_id=(ring(k), me), device_id_type=MESH)

        for k in range(1, NY):
            pl.semaphore_signal(barrier, inc=1, device_id=(lax.rem(y + k, NY) * NZ + z, me), device_id_type=MESH)
        for k in range(1, NM):
            pl.semaphore_signal(barrier, inc=1, device_id=(dp, lax.rem(me + k, NM)), device_id_type=MESH)

    weights_in.start()

    with jax.named_scope("gelu"):
        x_in.wait()
        cot_in.wait()
        pre = x_ref[...]
        act = 0.5 * pre * (1.0 + lax.erf(pre * 0.7071067811865476))
        ac[me] = act.T
        at[me, 0] = ac[me, pl.ds(pl.multiple_of(8 * z, 8), 8), :]
        cot = cot_ref[...]
        cot_t = jnp.concatenate([cot, jnp.zeros_like(cot)], axis=1).T[:64]
        ct[z] = cot_t

    with jax.named_scope("barwait"):
        pl.semaphore_wait(barrier, NZ - 1 + NY - 1 + NM - 1)

    def offset(j):
        half = lax.div(j + 1, 2)
        return half * (2 * lax.rem(j, 2) - 1)

    def to_ring(j):
        there = lax.rem(z + offset(j) + NZ, NZ)
        rows = pl.ds(pl.multiple_of(8 * there, 8), 8)
        return remote(ac.at[me, rows], at.at[me, j], za, j, j, y * NZ + there, me)

    def across_x(k):
        return remote(ac.at[me], ac.at[me], acx, k, k, dp, across(k))

    def to_mate(k):
        block = across(-k)
        return remote(ac.at[block], ac.at[block], acp, k, k, dp, mate)

    def part_across_x(p, k):
        part = at.at[me, pl.ds(HALF * p, HALF)]
        return remote(part, part, atx, NX * p + k, NX * p + k, dp, across(k))

    def part_to_mate(p, k):
        part = at.at[across(-k), pl.ds(HALF * p, HALF)]
        return remote(part, part, atp, NX * p + k, NX * p + k, dp, mate)

    RIGHT, LEFT = NZ // 2, NZ // 2 - 1
    TALL = 64 // CHUNKS

    def rightward(s, q):
        part = ct.at[lax.rem(z - s + 1 + NZ, NZ), pl.ds(TALL * q, TALL)]
        return remote(part, part, cr, CHUNKS * s + q, CHUNKS * s + q, ring(1), me)

    def leftward(s, q):
        part = ct.at[lax.rem(z + s - 1, NZ), pl.ds(TALL * q, TALL)]
        return remote(part, part, cl, CHUNKS * s + q, CHUNKS * s + q, ring(-1), me)

    for q in range(CHUNKS):
        rightward(1, q).start()
        leftward(1, q).start()

    def send_channels(first, end):
        @pl.loop(first, end)
        def _(j):
            to_ring(j).start()

    send_channels(1, HALF)

    def mates_share(k):
        return remote(ig.at[2 * k + 1 - c], rp.at[k], rps, k, k, dp, mate)

    def prepare_weights():
        weights_in.wait()
        for t in range(TAPS):
            high, low = halves(wv[t])
            wh[64 * t : 64 * t + 64, :] = high
            wl[64 * t : 64 * t + 64, :] = low
        wh[64 * TAPS :, :] = jnp.zeros_like(wh[64 * TAPS :, :])
        wl[64 * TAPS :, :] = jnp.zeros_like(wl[64 * TAPS :, :])

    def partial_sums():
        stack_t = halves(stacked_taps(ct[z]).T)
        for m in range(0, NM, 2):
            span = slice(CD * m, CD * m + 2 * CD)
            pair = dot3(stack_t, (wh[:, span], wl[:, span]), NN)
            ig[m] = pair[:, :CD]
            ig[m + 1] = pair[:, CD:]
        for k in range(NX):
            mates_share(k).start()

    def start_part(p):
        @pl.loop(max(1, HALF * p), HALF * (p + 1))
        def _(j):
            to_ring(j).wait_recv()

        for k in range(1, NX):
            part_across_x(p, k).start()
        part_to_mate(p, 0).start()

    def pass_part(p):
        for k in range(1, NX):
            part_across_x(p, k).wait_recv()
            part_to_mate(p, k).start()

    def part_here(p):
        for k in range(NX):
            part_to_mate(p, k).wait_recv()

    def start_activations():
        for k in range(1, NX):
            across_x(k).start()
        to_mate(0).start()

    def pass_activations():
        for k in range(1, NX):
            across_x(k).wait_recv()
            to_mate(k).start()

    def share(k):
        own = across(k)
        return remote(ig.at[own], rx.at[x], rxs, k, k, dp, own)

    def add_shares():
        for k in range(NX):
            mates_share(k).wait_recv()
            ig[2 * k + c] = ig[2 * k + c] + rp[k]

    def start_shares():
        for k in range(1, NX):
            share(k).start()

    def stacks(first, end):
        @pl.loop(first, end)
        def _(j):
            sh[j], sl[j] = halves(stacked_taps(ct[lax.rem(z - offset(j) + NZ, NZ)]))

    def leaves(first, end):
        @pl.loop(first, end)
        def _(j):
            channels = halves(at[:, j].reshape(CG, PIX))
            lt[lax.rem(z - offset(j) + NZ, NZ)] = dot3_joined(channels, (sh[j], sl[j]), NT) * (1.0 / PIX)

    last = CHUNKS - 1
    if NZ == 16:
        plan = {
            (1, 1): [(send_channels, HALF, NZ)],
            (1, last): [(prepare_weights,), (stacks, 0, 1)],
            (2, 0): [(start_part, 0)],
            (2, last): [(stacks, 1, 3)],
            (3, last): [(partial_sums,)],
            (4, 0): [(start_part, 1), (stacks, 3, 5)],
            (4, last): [(pass_part, 0), (stacks, 5, 7)],
            (5, last): [(part_here, 0), (leaves, 0, 5), (add_shares,), (start_activations,), (start_shares,)],
            (6, last): [(pass_part, 1), (leaves, 5, 7), (stacks, 7, 11), (leaves, 7, 8)],
            (7, last): [(part_here, 1), (leaves, 8, 11), (stacks, 11, 15), (leaves, 11, 15)],
            (8, last): [(stacks, 15, 16), (leaves, 15, 16)],
        }
    else:
        plan = {
            (RIGHT, last): [
                (send_channels, HALF, NZ), (prepare_weights,), (partial_sums,),
                (start_part, 0), (add_shares,), (start_part, 1), (start_activations,), (start_shares,),
                (pass_part, 0), (part_here, 0), (pass_part, 1), (part_here, 1), (stacks, 0, NZ), (leaves, 0, NZ),
            ],
        }

    for s in range(1, RIGHT + 1):
        for q in range(CHUNKS):
            with jax.named_scope(f"wait{s}_{q}"):
                rightward(s, q).wait_recv()
                if s < RIGHT:
                    rightward(s + 1, q).start()
                if s <= LEFT:
                    leftward(s, q).wait_recv()
                    if s < LEFT:
                        leftward(s + 1, q).start()
            for work in plan.get((s, q), []):
                with jax.named_scope(f"{work[0].__name__}{work[1] if len(work) > 1 else 0}"):
                    work[0](*work[1:])

    def exchange(buf, n, mine, sems, device, between=None):
        there = lambda k: lax.rem(mine + k, n)

        @pl.loop(1, n)
        def _(k):
            remote(buf.at[mine], buf.at[mine], sems, k, k, *device(there(k))).start()

        if between is not None:
            between()

        @pl.loop(1, n)
        def _(k):
            remote(buf.at[mine], buf.at[there(n - k)], sems, k, k, *device(there(k))).wait_recv()

        total = buf[0]
        for k in range(1, n):
            total = total + buf[k]
        return total

    def sent(n, buf, mine, sems, device):
        there = lambda k: lax.rem(mine + k, n)

        @pl.loop(1, n)
        def _(k):
            remote(buf.at[mine], buf.at[mine], sems, k, k, *device(there(k))).wait_send()

    on_mp = lambda k: (dp, k)
    on_z = lambda k: (y * NZ + k, me)
    on_y_mp = lambda k: (lax.div(k, NM) * NZ + z, lax.rem(k, NM))

    leave = lambda src, dst, k: pltpu.make_async_copy(src, dst, osem.at[k])

    def convolve():
        for k in range(NX):
            to_mate(k).wait_recv()
        full = halves(ac[...].reshape(NM * CD, PIX))
        total = None
        for t in range(TAPS):
            rows = slice(64 * t, 64 * t + 64)
            product = dot3((wh[rows, :], wl[rows, :]), full, NN)
            moved = shifted(product, t // 3 - 1, t % 3 - 1)
            total = moved if total is None else total + moved
        total = jnp.concatenate([total, jnp.zeros_like(total)], axis=0).T
        out_ref[...] = total[:, :64]
        leave(out_ref, out_hbm, 0).start()

    def finish_shares():
        total = ig[me]
        for k in range(1, NX):
            share(k).wait_recv()
            total = total + rx[lax.rem(x - k + NX, NX)]
        ig_ref[...] = total * gelu_slope(x_ref[...])
        leave(ig_ref, ig_hbm, 1).start()

    with jax.named_scope("gram16"):
        gm[me] = packed(gram(lt, NZ, CG), NZ)
    with jax.named_scope("g16mp"):
        gz[z] = exchange(gm, NM, me, gms, on_mp, pass_activations)
    with jax.named_scope("g16z"):
        table = exchange(gz, NZ, z, gzs, on_z, convolve)
    with jax.named_scope("coef16"):
        table = unpacked(table, NZ, cb)
        rows = table.shape[0]
        cb[0:rows, :] = coefficients(table, NZ)
    with jax.named_scope("comb16"):
        total = None
        for i in range(NZ):
            scale = jnp.concatenate([cb[i : i + 1, :]] * (STACK // 128), axis=1)
            term = lt[i] * scale
            total = term if total is None else total + term
        bt[...] = total
        yb[y] = bt[pl.ds(pl.multiple_of(QUARTER * y, 8), QUARTER), :]

    def to_y(k):
        there = lax.rem(y + k, NY)
        rows = pl.ds(pl.multiple_of(QUARTER * there, 8), QUARTER)
        return remote(bt.at[rows], yb.at[y], ys, k, k, there * NZ + z, me)

    with jax.named_scope("ywait"):
        for k in range(1, NY):
            to_y(k).start()
        for k in range(1, NY):
            to_y(k).wait_recv()

    def group(j):
        m, tap = divmod(j, TAPS)
        number = NZ * NM * tap + NZ * ((QUARTER // 8) * y + m) + z
        return lax.div(number, GROUPS), lax.rem(number, GROUPS)

    lower = lax.broadcasted_iota(jnp.int32, (8, 128), 1) < 64

    def send_groups():
        with jax.named_scope("permsend"):
            for j in range(GROUPS):
                m, tap = divmod(j, TAPS)
                span = slice(128 * (tap // 2), 128 * (tap // 2) + 128)
                for h in range(NY // 2):
                    left = yb[2 * h, 8 * m : 8 * m + 8, span]
                    right = yb[2 * h + 1, 8 * m : 8 * m + 8, span]
                    if tap % 2:
                        left = pltpu.roll(left, 64, 1)
                    else:
                        right = pltpu.roll(right, 64, 1)
                    pk[j, 8 * h : 8 * h + 8, :] = jnp.where(lower, left, right)
            for j in range(GROUPS):
                owner, slot = group(j)

                @pl.when(owner != dp)
                def _():
                    remote(pk.at[j], ob.at[slot], ps, j, slot, owner, me).start()

                @pl.when(owner == dp)
                def _():
                    pltpu.make_async_copy(pk.at[j], ob.at[slot], ps.at[1, slot]).start()

    def settle():
        finish_shares()

        @pl.loop(1, NZ)
        def _(j):
            to_ring(j).wait_send()

        for q in range(CHUNKS):
            for s in range(1, RIGHT + 1):
                rightward(s, q).wait_send()
            for s in range(1, LEFT + 1):
                leftward(s, q).wait_send()
        for k in range(NX):
            if k:
                across_x(k).wait_send()
                share(k).wait_send()
                for p in range(2):
                    part_across_x(p, k).wait_send()
            to_mate(k).wait_send()
            mates_share(k).wait_send()
            for p in range(2):
                part_to_mate(p, k).wait_send()
        for k in range(1, NY):
            to_y(k).wait_send()
        sent(NM, gm, me, gms, on_mp)
        sent(NZ, gz, z, gzs, on_z)

    with jax.named_scope("gram4"):
        here = NM * y + me
        hm[here] = packed(gram(yb, NY, QUARTER), NY)
    with jax.named_scope("g4ymp"):
        hz[z] = exchange(hm, NY * NM, here, hms, on_y_mp, send_groups)
    with jax.named_scope("g4z"):
        table = exchange(hz, NZ, z, hzs, on_z, settle)
    with jax.named_scope("coef4"):
        table = unpacked(table, NY, cb)
        cb[0:8, :] = coefficients(table, NY)
        scales = [jnp.where(lower, cb[2 * h : 2 * h + 1, :], cb[2 * h + 1 : 2 * h + 2, :]) for h in range(NY // 2)]
    with jax.named_scope("permrecv"):
        pieces = []
        for s in range(GROUPS):
            pltpu.make_async_copy(ob.at[s], ob.at[s], ps.at[1, s]).wait()
            piece = None
            for h in range(NY // 2):
                term = ob[s, 8 * h : 8 * h + 8, :] * scales[h]
                piece = term if piece is None else piece + term
            pieces.append(piece)
        columns = jnp.concatenate(pieces, axis=0)
        columns = columns + pltpu.roll(columns, 64, 1)
        fill = -8 * GROUPS % 128
        columns = jnp.concatenate([columns, jnp.zeros((fill, 128), F32)], axis=0).T
        wg_ref[...] = columns[:64, : 8 * GROUPS]
        leave(wg_ref, wg_hbm, 2).start()

    with jax.named_scope("drain"):
        leave(out_ref, out_hbm, 0).wait()
        leave(ig_ref, ig_hbm, 1).wait()
        leave(wg_ref, wg_hbm, 2).wait()
        sent(NY * NM, hm, here, hms, on_y_mp)
        sent(NZ, hz, z, hzs, on_z)
        for j in range(GROUPS):
            owner, slot = group(j)

            @pl.when(owner != dp)
            def _():
                remote(pk.at[j], ob.at[slot], ps, j, slot, owner, me).wait_send()


def local(NY, NZ, NX, preact, weights, cotangent):
    NM = 2 * NX
    CD = preact.shape[3]
    CG = 8 * NM
    QUARTER = CG // NY
    GROUPS = TAPS * NM // NY
    rows16 = NZ // min(NZ, 128 // NZ)
    vmem = lambda *shape: pltpu.VMEM(shape, F32)
    sems = lambda n: pltpu.SemaphoreType.DMA((2, n))
    anywhere = pl.BlockSpec(memory_space=pl.ANY)
    output, input_grad, weight_grad = pl.pallas_call(
        functools.partial(kernel, NY, NZ, NX),
        out_shape=[
            jax.ShapeDtypeStruct((PIX, 64), F32),
            jax.ShapeDtypeStruct((PIX, CD), F32),
            jax.ShapeDtypeStruct((64, 8 * GROUPS), F32),
        ],
        in_specs=[anywhere] * 3,
        out_specs=[anywhere] * 3,
        scratch_shapes=[
            vmem(PIX, CD),
            vmem(PIX, 64),
            vmem(PIX, 64),
            vmem(PIX, CD),
            vmem(64, 8 * GROUPS),
            vmem(TAPS, 64, NM * CD),
            pltpu.VMEM((STACK, NM * CD), BF16),
            pltpu.VMEM((STACK, NM * CD), BF16),
            vmem(NM, CD, PIX),
            vmem(NM, NZ, 8, PIX),
            vmem(NZ, 64, PIX),
            vmem(NM, PIX, CD),
            vmem(NX, PIX, CD),
            vmem(NX, PIX, CD),
            pltpu.VMEM((NZ, STACK, PIX), BF16),
            pltpu.VMEM((NZ, STACK, PIX), BF16),
            vmem(NZ, CG, STACK),
            vmem(16, 128),
            vmem(CG, STACK),
            vmem(NY, QUARTER, STACK),
            vmem(GROUPS, 4 * NY, 128),
            vmem(GROUPS, 4 * NY, 128),
            vmem(NM, rows16, 128),
            vmem(NZ, rows16, 128),
            vmem(NY * NM, 1, 128),
            vmem(NZ, 1, 128),
            pltpu.SemaphoreType.DMA((3,)),
            pltpu.SemaphoreType.DMA((3,)),
            sems(NZ), sems(CHUNKS * NZ), sems(CHUNKS * NZ),
            sems(NX), sems(NX), sems(2 * NX), sems(2 * NX), sems(NX), sems(NX),
            sems(NM), sems(NZ), sems(NY), sems(NY * NM), sems(NZ),
            sems(GROUPS),
        ],
        compiler_params=pltpu.CompilerParams(collective_id=0, has_side_effects=True),
        name="step",
    )(preact.reshape(PIX, CD), cotangent.reshape(PIX, 64), weights.transpose(1, 0, 2))
    def hand_over(a, b, d, e, f, g):
        e[...] = a[...]
        f[...] = b[...]
        g[...] = d[...]

    whole = pl.BlockSpec(memory_space=pltpu.VMEM)
    output, input_grad, weight_grad = pl.pallas_call(
        hand_over,
        out_shape=[jax.ShapeDtypeStruct(v.shape, F32) for v in (output, input_grad, weight_grad)],
        in_specs=[whole] * 3,
        out_specs=[whole] * 3,
        name="hand_over",
    )(output, input_grad, weight_grad)
    return output.reshape(1, SIDE, SIDE, 64), input_grad.reshape(preact.shape), weight_grad


def build(mesh, NY, NZ, NX):
    placed = (P("dp", None, None, "mp"), P("mp", None, None), P("dp", None, None, "mp"))
    return jax.shard_map(
        functools.partial(local, NY, NZ, NX),
        mesh=mesh,
        in_specs=placed,
        out_specs=(P("dp", None, None, "mp"), P("dp", None, None, "mp"), P("mp", "dp")),
        check_vma=False,
    )


def solution(mesh):
    return build(mesh, 4, mesh.shape["dp"] // 4, mesh.shape["mp"] // 2)
```

```python
import functools

import jax
import jax.numpy as jnp
from jax import lax
from jax.experimental import pallas as pl
from jax.experimental.pallas import tpu as pltpu
from jax.sharding import PartitionSpec as P

MESH = pl.DeviceIdType.MESH
F32 = jnp.float32
BF16 = jnp.bfloat16
EPS = 1e-06
SIDE = 16
PIX = SIDE * SIDE
TAPS = 9
STACK = 640


def halves(values):
    high = values.astype(BF16)
    low = (values - high.astype(F32)).astype(BF16)
    return high, low


def dot3(a, b, dims):
    one = lambda p, q: lax.dot_general(p, q, (dims, ((), ())), preferred_element_type=F32)
    return one(a[0], b[0]) + (one(a[0], b[1]) + one(a[1], b[0]))


def dot3_joined(a, b, dims):
    one = lambda p, q: lax.dot_general(p, q, (dims, ((), ())), preferred_element_type=F32)
    rows = a[0].shape[0]
    both = one(jnp.concatenate(a, axis=0), b[0])
    return both[:rows] + (both[rows:] + one(a[0], b[1]))


NN = ((1,), (0,))
NT = ((1,), (1,))


def shifted(values, dy, dx):
    pixel = lax.broadcasted_iota(jnp.int32, values.shape, 1)
    column = jnp.bitwise_and(pixel, SIDE - 1)
    inside = None
    if dx:
        inside = (column >= 1) if dx < 0 else (column < SIDE - 1)
    if dy:
        rows = (pixel >= SIDE) if dy < 0 else (pixel < PIX - SIDE)
        inside = rows if inside is None else jnp.logical_and(inside, rows)
    step = SIDE * dy + dx
    if step == 0:
        return values
    return jnp.where(inside, pltpu.roll(values, (-step) % PIX, 1), 0.0)


def stacked_taps(cot):
    taps = [shifted(cot, 1 - t // 3, 1 - t % 3) for t in range(TAPS)]
    return jnp.concatenate(taps + [jnp.zeros_like(cot)], axis=0)


def folded(total, n, bits):
    size = 1 << bits
    sub = lax.broadcasted_iota(jnp.int32, total.shape, 0)
    lane = lax.broadcasted_iota(jnp.int32, total.shape, 1)
    kept = jnp.where(jnp.bitwise_and(sub, size - 1) == jnp.bitwise_and(lane, size - 1), total, 0.0)
    kept = jnp.sum(kept.reshape(n, size, size * n), axis=1)
    source = lax.broadcasted_iota(jnp.int32, (size * n, 128), 0)
    target = lax.broadcasted_iota(jnp.int32, (size * n, 128), 1)
    fold = jnp.where(jnp.right_shift(source, bits) == target, 1.0, 0.0).astype(F32)
    return lax.dot_general(kept, fold, (NN, ((), ())), preferred_element_type=F32, precision=lax.Precision.HIGHEST)


def gram(ref, n, rows):
    total = None
    for r in range(rows // 8):
        block = halves(ref[:, 8 * r : 8 * r + 8, :].reshape(8 * n, STACK))
        both = jnp.concatenate(block, axis=0)
        part = lax.dot_general(both, block[0], (NT, ((), ())), preferred_element_type=F32)
        total = part if total is None else total + part
    low = total[8 * n :]
    return folded(total[: 8 * n] + (low + low.T), n, 3)


def packed(table, n):
    per = min(n, 128 // n)
    rows = []
    for r in range(n // per):
        row = table[r * per : r * per + 1]
        for i in range(1, per):
            row = row + pltpu.roll(table[r * per + i : r * per + i + 1], n * i, 1)
        rows.append(row)
    return rows[0] if len(rows) == 1 else jnp.concatenate(rows, axis=0)


def unpacked(rows, n, scratch):
    per = min(n, 128 // n)
    held = max(n, 8)
    if n < 8:
        scratch[0:8, :] = jnp.zeros((8, 128), F32)
    for i in range(n):
        row = rows[i // per : i // per + 1]
        scratch[i : i + 1, :] = pltpu.roll(row, (128 - n * (i % per)) % 128, 1) if i % per else row
    return scratch[0:held, :]


def coefficients(table, n):
    rows = table.shape[0]
    sub = lax.broadcasted_iota(jnp.int32, table.shape, 0)
    lane = lax.broadcasted_iota(jnp.int32, table.shape, 1)
    diagonal = sub == lane
    result = jnp.ones((rows, 1), F32)
    b = 1
    while b < n:
        partner = jnp.bitwise_xor(sub, b) == lane
        own = jnp.where(diagonal, table, 0.0)
        cross = jnp.where(partner, table, 0.0)
        down = 1.0 - jnp.sum(cross, 1, keepdims=True) / (2.0 * (jnp.sum(own, 1, keepdims=True) + EPS))
        along = 1.0 - jnp.sum(cross, 0, keepdims=True) / (2.0 * (jnp.sum(own, 0, keepdims=True) + EPS))
        result = result * down
        if 2 * b < n:
            table = table * down * along
            moved = jnp.where(jnp.bitwise_and(sub, b) != 0, pltpu.roll(table, b, 0), pltpu.roll(table, rows - b, 0))
            table = table + moved
            moved = jnp.where(jnp.bitwise_and(lane, b) != 0, pltpu.roll(table, b, 1), pltpu.roll(table, 128 - b, 1))
            table = table + moved
        b *= 2
    return jnp.broadcast_to(result, (rows, 128))


def gelu_slope(values):
    return (
        0.5 * (1.0 + lax.erf(values * 0.7071067811865476))
        + values * jnp.exp(-0.5 * values * values) * 0.3989422804014327
    )


CHUNKS = 2
LIMIT = 54500 * 1024


def kernel(
    NY, NZ, NX,
    x_hbm, cot_hbm, w_hbm,
    out_ref, ig_ref, wg_ref,
    x_ref, cot_ref, wv, wh, wl, ac, at, ct, ig, rp, rx, sh, sl, lt, cb, bt, yb, pk, ob, gm, gz, hm, hz,
    isem, za, cr, cl, acx, acp, atx, atp, rps, rxs, gms, gzs, ys, hms, hzs, ps,
):
    NM = 2 * NX
    CD = x_ref.shape[1]
    CG = 8 * NM
    GROUPS = TAPS * NM // NY
    QUARTER = CG // NY
    HALF = NZ // 2
    dp = lax.axis_index("dp")
    me = lax.axis_index("mp")
    y, z = lax.div(dp, NZ), lax.rem(dp, NZ)
    x, c = lax.div(me, 2), lax.rem(me, 2)
    mate = me + 1 - 2 * c
    ring = lambda k: y * NZ + lax.rem(z + k + NZ, NZ)
    across = lambda k: 2 * lax.rem(x + k + NX, NX) + c

    def remote(src, dst, sems, k, r, to_dp, to_mp):
        return pltpu.make_async_remote_copy(
            src_ref=src, dst_ref=dst, send_sem=sems.at[0, k], recv_sem=sems.at[1, r],
            device_id=(to_dp, to_mp), device_id_type=MESH,
        )

    x_in = pltpu.make_async_copy(x_hbm, x_ref, isem.at[0])
    cot_in = pltpu.make_async_copy(cot_hbm, cot_ref, isem.at[1])
    weights_in = pltpu.make_async_copy(w_hbm, wv, isem.at[2])
    x_in.start()
    cot_in.start()

    with jax.named_scope("signals"):
        barrier = pltpu.get_barrier_semaphore()

        @pl.loop(1, NZ)
        def _(k):
            pl.semaphore_signal(barrier, inc=1, device_id=(ring(k), me), device_id_type=MESH)

        for k in range(1, NY):
            pl.semaphore_signal(barrier, inc=1, device_id=(lax.rem(y + k, NY) * NZ + z, me), device_id_type=MESH)
        for k in range(1, NM):
            pl.semaphore_signal(barrier, inc=1, device_id=(dp, lax.rem(me + k, NM)), device_id_type=MESH)

    weights_in.start()

    with jax.named_scope("gelu"):
        x_in.wait()
        cot_in.wait()
        pre = x_ref[...]
        act = 0.5 * pre * (1.0 + lax.erf(pre * 0.7071067811865476))
        ac[me] = act.T
        at[me, 0] = ac[me, pl.ds(pl.multiple_of(8 * z, 8), 8), :]
        cot = cot_ref[...]
        cot_t = jnp.concatenate([cot, jnp.zeros_like(cot)], axis=1).T[:64]
        ct[z] = cot_t

    with jax.named_scope("prepare"):
        weights_in.wait()
        for t in range(TAPS):
            high, low = halves(wv[t])
            wh[64 * t : 64 * t + 64, :] = high
            wl[64 * t : 64 * t + 64, :] = low
        wh[64 * TAPS :, :] = jnp.zeros_like(wh[64 * TAPS :, :])
        wl[64 * TAPS :, :] = jnp.zeros_like(wl[64 * TAPS :, :])
        stack = stacked_taps(cot_t)
        sh[0], sl[0] = halves(stack)
        stack_t = halves(stack.T)
        for m in range(0, NM, 2):
            span = slice(CD * m, CD * m + 2 * CD)
            pair = dot3(stack_t, (wh[:, span], wl[:, span]), NN)
            ig[m] = pair[:, :CD]
            ig[m + 1] = pair[:, CD:]

    with jax.named_scope("barwait"):
        pl.semaphore_wait(barrier, NZ - 1 + NY - 1 + NM - 1)

    def offset(j):
        half = lax.div(j + 1, 2)
        return half * (2 * lax.rem(j, 2) - 1)

    def to_ring(j):
        there = lax.rem(z + offset(j) + NZ, NZ)
        rows = pl.ds(pl.multiple_of(8 * there, 8), 8)
        return remote(ac.at[me, rows], at.at[me, j], za, j, j, y * NZ + there, me)

    def across_x(k):
        return remote(ac.at[me], ac.at[me], acx, k, k, dp, across(k))

    def to_mate(k):
        block = across(-k)
        return remote(ac.at[block], ac.at[block], acp, k, k, dp, mate)

    def part_across_x(p, k):
        part = at.at[me, pl.ds(HALF * p, HALF)]
        return remote(part, part, atx, NX * p + k, NX * p + k, dp, across(k))

    def part_to_mate(p, k):
        part = at.at[across(-k), pl.ds(HALF * p, HALF)]
        return remote(part, part, atp, NX * p + k, NX * p + k, dp, mate)

    RIGHT, LEFT = NZ // 2, NZ // 2 - 1
    TALL = 64 // CHUNKS

    def rightward(s, q):
        part = ct.at[lax.rem(z - s + 1 + NZ, NZ), pl.ds(TALL * q, TALL)]
        return remote(part, part, cr, CHUNKS * s + q, CHUNKS * s + q, ring(1), me)

    def leftward(s, q):
        part = ct.at[lax.rem(z + s - 1, NZ), pl.ds(TALL * q, TALL)]
        return remote(part, part, cl, CHUNKS * s + q, CHUNKS * s + q, ring(-1), me)

    for q in range(CHUNKS):
        rightward(1, q).start()
        leftward(1, q).start()

    def send_channels(first, end):
        @pl.loop(first, end)
        def _(j):
            to_ring(j).start()

    send_channels(1, HALF)

    def mates_share(k):
        return remote(ig.at[2 * k + 1 - c], rp.at[k], rps, k, k, dp, mate)

    for k in range(NX):
        mates_share(k).start()

    def start_part(p):
        @pl.loop(max(1, HALF * p), HALF * (p + 1))
        def _(j):
            to_ring(j).wait_recv()

        for k in range(1, NX):
            part_across_x(p, k).start()
        part_to_mate(p, 0).start()

    def pass_part(p):
        for k in range(1, NX):
            part_across_x(p, k).wait_recv()
            part_to_mate(p, k).start()

    def part_here(p):
        for k in range(NX):
            part_to_mate(p, k).wait_recv()

    def start_activations():
        for k in range(1, NX):
            across_x(k).start()
        to_mate(0).start()

    def pass_activations():
        for k in range(1, NX):
            across_x(k).wait_recv()
            to_mate(k).start()

    def share(k):
        own = across(k)
        return remote(ig.at[own], rx.at[x], rxs, k, k, dp, own)

    def add_shares():
        for k in range(NX):
            mates_share(k).wait_recv()
            ig[2 * k + c] = ig[2 * k + c] + rp[k]

    def start_shares():
        for k in range(1, NX):
            share(k).start()

    def stacks(first, end):
        @pl.loop(first, end)
        def _(j):
            sh[j], sl[j] = halves(stacked_taps(ct[lax.rem(z - offset(j) + NZ, NZ)]))

    def leaves(first, end):
        @pl.loop(first, end)
        def _(j):
            channels = halves(at[:, j].reshape(CG, PIX))
            lt[lax.rem(z - offset(j) + NZ, NZ)] = dot3_joined(channels, (sh[j], sl[j]), NT) * (1.0 / PIX)

    last = CHUNKS - 1
    if NZ == 16:
        plan = {
            (1, 1): [(send_channels, HALF, NZ)],
            (2, 0): [(start_part, 0)],
            (2, 3): [(stacks, 1, 3)],
            (3, 3): [(stacks, 3, 5)],
            (4, 0): [(start_part, 1)],
            (4, 2): [(pass_part, 0)],
            (4, 3): [(stacks, 5, 7)],
            (5, 1): [(part_here, 0)],
            (5, 3): [(leaves, 0, 5), (add_shares,), (start_activations,), (start_shares,)],
            (6, 1): [(pass_part, 1)],
            (6, 3): [(stacks, 7, 11), (leaves, 5, 8)],
            (7, 3): [(part_here, 1), (stacks, 11, 15), (leaves, 8, 15)],
            (8, 3): [(stacks, 15, 16), (leaves, 15, 16)],
        }
    else:
        plan = {
            (RIGHT, last): [
                (send_channels, HALF, NZ),
                (start_part, 0), (add_shares,), (start_part, 1), (start_activations,), (start_shares,),
                (pass_part, 0), (part_here, 0), (pass_part, 1), (part_here, 1), (stacks, 1, NZ), (leaves, 0, NZ),
            ],
        }

    merged = {}
    for (s, q), works in plan.items():
        merged.setdefault((s, q // 2 if NZ == 16 else q), []).extend(works)
    plan = merged

    for s in range(1, RIGHT + 1):
        for q in range(CHUNKS):
            with jax.named_scope(f"wait{s}_{q}"):
                rightward(s, q).wait_recv()
                if s < RIGHT:
                    rightward(s + 1, q).start()
                if s <= LEFT:
                    leftward(s, q).wait_recv()
                    if s < LEFT:
                        leftward(s + 1, q).start()
            for work in plan.get((s, q), []):
                with jax.named_scope(f"{work[0].__name__}{work[1] if len(work) > 1 else 0}"):
                    work[0](*work[1:])

    def exchange(buf, n, mine, sems, device, between=None):
        there = lambda k: lax.rem(mine + k, n)

        @pl.loop(1, n)
        def _(k):
            remote(buf.at[mine], buf.at[mine], sems, k, k, *device(there(k))).start()

        if between is not None:
            between()

        @pl.loop(1, n)
        def _(k):
            remote(buf.at[mine], buf.at[there(n - k)], sems, k, k, *device(there(k))).wait_recv()

        total = buf[0]
        for k in range(1, n):
            total = total + buf[k]
        return total

    def sent(n, buf, mine, sems, device):
        there = lambda k: lax.rem(mine + k, n)

        @pl.loop(1, n)
        def _(k):
            remote(buf.at[mine], buf.at[mine], sems, k, k, *device(there(k))).wait_send()

    on_mp = lambda k: (dp, k)
    on_z = lambda k: (y * NZ + k, me)
    on_y_mp = lambda k: (lax.div(k, NM) * NZ + z, lax.rem(k, NM))

    def convolve():
        for k in range(NX):
            to_mate(k).wait_recv()
        full = halves(ac[...].reshape(NM * CD, PIX))
        total = None
        for t in range(TAPS):
            rows = slice(64 * t, 64 * t + 64)
            product = dot3((wh[rows, :], wl[rows, :]), full, NN)
            moved = shifted(product, t // 3 - 1, t % 3 - 1)
            total = moved if total is None else total + moved
        total = jnp.concatenate([total, jnp.zeros_like(total)], axis=0).T
        out_ref[...] = total[:, :64]

    def finish_shares():
        total = ig[me]
        for k in range(1, NX):
            share(k).wait_recv()
            total = total + rx[lax.rem(x - k + NX, NX)]
        ig_ref[...] = total * gelu_slope(x_ref[...])

    with jax.named_scope("gram16"):
        gm[me] = packed(gram(lt, NZ, CG), NZ)
    with jax.named_scope("g16mp"):
        gz[z] = exchange(gm, NM, me, gms, on_mp, pass_activations)
    with jax.named_scope("g16z"):
        table = exchange(gz, NZ, z, gzs, on_z, convolve)
    with jax.named_scope("coef16"):
        table = unpacked(table, NZ, cb)
        rows = table.shape[0]
        cb[0:rows, :] = coefficients(table, NZ)
    with jax.named_scope("comb16"):
        total = None
        for i in range(NZ):
            scale = jnp.concatenate([cb[i : i + 1, :]] * (STACK // 128), axis=1)
            term = lt[i] * scale
            total = term if total is None else total + term
        bt[...] = total
        yb[y] = bt[pl.ds(pl.multiple_of(QUARTER * y, 8), QUARTER), :]

    def to_y(k):
        there = lax.rem(y + k, NY)
        rows = pl.ds(pl.multiple_of(QUARTER * there, 8), QUARTER)
        return remote(bt.at[rows], yb.at[y], ys, k, k, there * NZ + z, me)

    with jax.named_scope("ywait"):
        for k in range(1, NY):
            to_y(k).start()
        for k in range(1, NY):
            to_y(k).wait_recv()

    def group(j):
        m, tap = divmod(j, TAPS)
        number = NZ * NM * tap + NZ * ((QUARTER // 8) * y + m) + z
        return lax.div(number, GROUPS), lax.rem(number, GROUPS)

    lower = lax.broadcasted_iota(jnp.int32, (8, 128), 1) < 64

    def send_groups():
        with jax.named_scope("permsend"):
            for j in range(GROUPS):
                m, tap = divmod(j, TAPS)
                span = slice(128 * (tap // 2), 128 * (tap // 2) + 128)
                for h in range(NY // 2):
                    left = yb[2 * h, 8 * m : 8 * m + 8, span]
                    right = yb[2 * h + 1, 8 * m : 8 * m + 8, span]
                    if tap % 2:
                        left = pltpu.roll(left, 64, 1)
                    else:
                        right = pltpu.roll(right, 64, 1)
                    pk[j, 8 * h : 8 * h + 8, :] = jnp.where(lower, left, right)
            for j in range(GROUPS):
                owner, slot = group(j)

                @pl.when(owner != dp)
                def _():
                    remote(pk.at[j], ob.at[slot], ps, j, slot, owner, me).start()

                @pl.when(owner == dp)
                def _():
                    pltpu.make_async_copy(pk.at[j], ob.at[slot], ps.at[1, slot]).start()

    def settle():
        finish_shares()

        @pl.loop(1, NZ)
        def _(j):
            to_ring(j).wait_send()

        for q in range(CHUNKS):
            for s in range(1, RIGHT + 1):
                rightward(s, q).wait_send()
            for s in range(1, LEFT + 1):
                leftward(s, q).wait_send()
        for k in range(NX):
            if k:
                across_x(k).wait_send()
                share(k).wait_send()
                for p in range(2):
                    part_across_x(p, k).wait_send()
            to_mate(k).wait_send()
            mates_share(k).wait_send()
            for p in range(2):
                part_to_mate(p, k).wait_send()
        for k in range(1, NY):
            to_y(k).wait_send()
        sent(NM, gm, me, gms, on_mp)
        sent(NZ, gz, z, gzs, on_z)

    with jax.named_scope("gram4"):
        here = NM * y + me
        hm[here] = packed(gram(yb, NY, QUARTER), NY)
    with jax.named_scope("g4ymp"):
        hz[z] = exchange(hm, NY * NM, here, hms, on_y_mp, send_groups)
    with jax.named_scope("g4z"):
        table = exchange(hz, NZ, z, hzs, on_z, settle)
    with jax.named_scope("coef4"):
        table = unpacked(table, NY, cb)
        cb[0:8, :] = coefficients(table, NY)
        scales = [jnp.where(lower, cb[2 * h : 2 * h + 1, :], cb[2 * h + 1 : 2 * h + 2, :]) for h in range(NY // 2)]
    with jax.named_scope("permrecv"):
        pieces = []
        for s in range(GROUPS):
            pltpu.make_async_copy(ob.at[s], ob.at[s], ps.at[1, s]).wait()
            piece = None
            for h in range(NY // 2):
                term = ob[s, 8 * h : 8 * h + 8, :] * scales[h]
                piece = term if piece is None else piece + term
            pieces.append(piece)
        columns = jnp.concatenate(pieces, axis=0)
        columns = columns + pltpu.roll(columns, 64, 1)
        fill = -8 * GROUPS % 128
        columns = jnp.concatenate([columns, jnp.zeros((fill, 128), F32)], axis=0).T
        wg_ref[...] = columns[:64, : 8 * GROUPS]

    with jax.named_scope("drain"):
        sent(NY * NM, hm, here, hms, on_y_mp)
        sent(NZ, hz, z, hzs, on_z)
        for j in range(GROUPS):
            owner, slot = group(j)

            @pl.when(owner != dp)
            def _():
                remote(pk.at[j], ob.at[slot], ps, j, slot, owner, me).wait_send()


def local(NY, NZ, NX, preact, weights, cotangent):
    NM = 2 * NX
    CD = preact.shape[3]
    CG = 8 * NM
    QUARTER = CG // NY
    GROUPS = TAPS * NM // NY
    rows16 = NZ // min(NZ, 128 // NZ)
    vmem = lambda *shape: pltpu.VMEM(shape, F32)
    sems = lambda n: pltpu.SemaphoreType.DMA((2, n))
    anywhere = pl.BlockSpec(memory_space=pl.ANY)
    output, input_grad, weight_grad = pl.pallas_call(
        functools.partial(kernel, NY, NZ, NX),
        out_shape=[
            jax.ShapeDtypeStruct((PIX, 64), F32),
            jax.ShapeDtypeStruct((PIX, CD), F32),
            jax.ShapeDtypeStruct((64, 8 * GROUPS), F32),
        ],
        in_specs=[anywhere] * 3,
        out_specs=[pl.BlockSpec(memory_space=pltpu.VMEM)] * 3,
        scratch_shapes=[
            vmem(PIX, CD),
            vmem(PIX, 64),
            vmem(TAPS, 64, NM * CD),
            pltpu.VMEM((STACK, NM * CD), BF16),
            pltpu.VMEM((STACK, NM * CD), BF16),
            vmem(NM, CD, PIX),
            vmem(NM, NZ, 8, PIX),
            vmem(NZ, 64, PIX),
            vmem(NM, PIX, CD),
            vmem(NX, PIX, CD),
            vmem(NX, PIX, CD),
            pltpu.VMEM((NZ, STACK, PIX), BF16),
            pltpu.VMEM((NZ, STACK, PIX), BF16),
            vmem(NZ, CG, STACK),
            vmem(16, 128),
            vmem(CG, STACK),
            vmem(NY, QUARTER, STACK),
            vmem(GROUPS, 4 * NY, 128),
            vmem(GROUPS, 4 * NY, 128),
            vmem(NM, rows16, 128),
            vmem(NZ, rows16, 128),
            vmem(NY * NM, 1, 128),
            vmem(NZ, 1, 128),
            pltpu.SemaphoreType.DMA((3,)),
            sems(NZ), sems(CHUNKS * NZ), sems(CHUNKS * NZ),
            sems(NX), sems(NX), sems(2 * NX), sems(2 * NX), sems(NX), sems(NX),
            sems(NM), sems(NZ), sems(NY), sems(NY * NM), sems(NZ),
            sems(GROUPS),
        ],
        compiler_params=pltpu.CompilerParams(collective_id=0, has_side_effects=True, vmem_limit_bytes=LIMIT),
        name="step",
    )(*(pltpu.with_memory_space_constraint(v, pltpu.HBM) for v in (preact.reshape(PIX, CD), cotangent.reshape(PIX, 64), weights.transpose(1, 0, 2))))
    def hand_over(a, b, d, e, f, g):
        e[...] = a[...]
        f[...] = b[...]
        g[...] = d[...]

    whole = pl.BlockSpec(memory_space=pltpu.VMEM)
    output, input_grad, weight_grad = pl.pallas_call(
        hand_over,
        out_shape=[jax.ShapeDtypeStruct(v.shape, F32) for v in (output, input_grad, weight_grad)],
        in_specs=[whole] * 3,
        out_specs=[whole] * 3,
        compiler_params=pltpu.CompilerParams(vmem_limit_bytes=2 * 2**20),
        name="hand_over",
    )(output, input_grad, weight_grad)
    return output.reshape(1, SIDE, SIDE, 64), input_grad.reshape(preact.shape), weight_grad


def build(mesh, NY, NZ, NX):
    placed = (P("dp", None, None, "mp"), P("mp", None, None), P("dp", None, None, "mp"))
    return jax.shard_map(
        functools.partial(local, NY, NZ, NX),
        mesh=mesh,
        in_specs=placed,
        out_specs=(P("dp", None, None, "mp"), P("dp", None, None, "mp"), P("mp", "dp")),
        check_vma=False,
    )


def solution(mesh):
    return build(mesh, 4, mesh.shape["dp"] // 4, mesh.shape["mp"] // 2)
```

```python
import functools

import jax
import jax.numpy as jnp
from jax import lax
from jax.experimental import pallas as pl
from jax.experimental.pallas import tpu as pltpu
from jax.sharding import PartitionSpec as P

MESH = pl.DeviceIdType.MESH
F32 = jnp.float32
BF16 = jnp.bfloat16
EPS = 1e-06
SIDE = 16
PIX = SIDE * SIDE
TAPS = 9
STACK = 640


def halves(values):
    high = values.astype(BF16)
    low = (values - high.astype(F32)).astype(BF16)
    return high, low


def dot3(a, b, dims):
    one = lambda p, q: lax.dot_general(p, q, (dims, ((), ())), preferred_element_type=F32)
    return one(a[0], b[0]) + (one(a[0], b[1]) + one(a[1], b[0]))


def dot3_joined(a, b, dims):
    one = lambda p, q: lax.dot_general(p, q, (dims, ((), ())), preferred_element_type=F32)
    rows = a[0].shape[0]
    both = one(jnp.concatenate(a, axis=0), b[0])
    return both[:rows] + (both[rows:] + one(a[0], b[1]))


NN = ((1,), (0,))
NT = ((1,), (1,))


def shifted(values, dy, dx):
    pixel = lax.broadcasted_iota(jnp.int32, values.shape, 1)
    column = jnp.bitwise_and(pixel, SIDE - 1)
    inside = None
    if dx:
        inside = (column >= 1) if dx < 0 else (column < SIDE - 1)
    if dy:
        rows = (pixel >= SIDE) if dy < 0 else (pixel < PIX - SIDE)
        inside = rows if inside is None else jnp.logical_and(inside, rows)
    step = SIDE * dy + dx
    if step == 0:
        return values
    return jnp.where(inside, pltpu.roll(values, (-step) % PIX, 1), 0.0)


def stacked_taps(cot):
    taps = [shifted(cot, 1 - t // 3, 1 - t % 3) for t in range(TAPS)]
    return jnp.concatenate(taps + [jnp.zeros_like(cot)], axis=0)


def folded(total, n, bits):
    size = 1 << bits
    sub = lax.broadcasted_iota(jnp.int32, total.shape, 0)
    lane = lax.broadcasted_iota(jnp.int32, total.shape, 1)
    kept = jnp.where(jnp.bitwise_and(sub, size - 1) == jnp.bitwise_and(lane, size - 1), total, 0.0)
    kept = jnp.sum(kept.reshape(n, size, size * n), axis=1)
    source = lax.broadcasted_iota(jnp.int32, (size * n, 128), 0)
    target = lax.broadcasted_iota(jnp.int32, (size * n, 128), 1)
    fold = jnp.where(jnp.right_shift(source, bits) == target, 1.0, 0.0).astype(F32)
    return lax.dot_general(kept, fold, (NN, ((), ())), preferred_element_type=F32, precision=lax.Precision.HIGHEST)


def gram(ref, n, rows):
    total = None
    for r in range(rows // 8):
        block = halves(ref[:, 8 * r : 8 * r + 8, :].reshape(8 * n, STACK))
        both = jnp.concatenate(block, axis=0)
        part = lax.dot_general(both, block[0], (NT, ((), ())), preferred_element_type=F32)
        total = part if total is None else total + part
    low = total[8 * n :]
    return folded(total[: 8 * n] + (low + low.T), n, 3)


def packed(table, n):
    per = min(n, 128 // n)
    rows = []
    for r in range(n // per):
        row = table[r * per : r * per + 1]
        for i in range(1, per):
            row = row + pltpu.roll(table[r * per + i : r * per + i + 1], n * i, 1)
        rows.append(row)
    return rows[0] if len(rows) == 1 else jnp.concatenate(rows, axis=0)


def unpacked(rows, n, scratch):
    per = min(n, 128 // n)
    held = max(n, 8)
    if n < 8:
        scratch[0:8, :] = jnp.zeros((8, 128), F32)
    for i in range(n):
        row = rows[i // per : i // per + 1]
        scratch[i : i + 1, :] = pltpu.roll(row, (128 - n * (i % per)) % 128, 1) if i % per else row
    return scratch[0:held, :]


def coefficients(table, n):
    rows = table.shape[0]
    sub = lax.broadcasted_iota(jnp.int32, table.shape, 0)
    lane = lax.broadcasted_iota(jnp.int32, table.shape, 1)
    diagonal = sub == lane
    result = jnp.ones((rows, 1), F32)
    b = 1
    while b < n:
        partner = jnp.bitwise_xor(sub, b) == lane
        own = jnp.where(diagonal, table, 0.0)
        cross = jnp.where(partner, table, 0.0)
        down = 1.0 - jnp.sum(cross, 1, keepdims=True) / (2.0 * (jnp.sum(own, 1, keepdims=True) + EPS))
        along = 1.0 - jnp.sum(cross, 0, keepdims=True) / (2.0 * (jnp.sum(own, 0, keepdims=True) + EPS))
        result = result * down
        if 2 * b < n:
            table = table * down * along
            moved = jnp.where(jnp.bitwise_and(sub, b) != 0, pltpu.roll(table, b, 0), pltpu.roll(table, rows - b, 0))
            table = table + moved
            moved = jnp.where(jnp.bitwise_and(lane, b) != 0, pltpu.roll(table, b, 1), pltpu.roll(table, 128 - b, 1))
            table = table + moved
        b *= 2
    return jnp.broadcast_to(result, (rows, 128))


def gelu_slope(values):
    return (
        0.5 * (1.0 + lax.erf(values * 0.7071067811865476))
        + values * jnp.exp(-0.5 * values * values) * 0.3989422804014327
    )


CHUNKS = 2
LIMIT = 54500 * 1024


def kernel(
    NY, NZ, NX,
    x_hbm, cot_hbm, w_hbm,
    out_ref, ig_ref, wg_ref,
    x_ref, cot_ref, wv, wh, wl, ac, at, ct, ig, rp, rx, sh, sl, lt, cb, bt, yb, pk, ob, gm, gz, hm, hz,
    isem, za, cr, cl, acx, acp, atx, atp, rps, rxs, gms, gzs, ys, hms, hzs, ps,
):
    NM = 2 * NX
    CD = x_ref.shape[1]
    CG = 8 * NM
    GROUPS = TAPS * NM // NY
    QUARTER = CG // NY
    HALF = NZ // 2
    dp = lax.axis_index("dp")
    me = lax.axis_index("mp")
    y, z = lax.div(dp, NZ), lax.rem(dp, NZ)
    x, c = lax.div(me, 2), lax.rem(me, 2)
    mate = me + 1 - 2 * c
    ring = lambda k: y * NZ + lax.rem(z + k + NZ, NZ)
    across = lambda k: 2 * lax.rem(x + k + NX, NX) + c

    def remote(src, dst, sems, k, r, to_dp, to_mp):
        return pltpu.make_async_remote_copy(
            src_ref=src, dst_ref=dst, send_sem=sems.at[0, k], recv_sem=sems.at[1, r],
            device_id=(to_dp, to_mp), device_id_type=MESH,
        )

    x_in = pltpu.make_async_copy(x_hbm, x_ref, isem.at[0])
    cot_in = pltpu.make_async_copy(cot_hbm, cot_ref, isem.at[1])
    weights_in = pltpu.make_async_copy(w_hbm, wv, isem.at[2])
    x_in.start()
    cot_in.start()

    with jax.named_scope("signals"):
        barrier = pltpu.get_barrier_semaphore()

        @pl.loop(1, NZ)
        def _(k):
            pl.semaphore_signal(barrier, inc=1, device_id=(ring(k), me), device_id_type=MESH)

        for k in range(1, NY):
            pl.semaphore_signal(barrier, inc=1, device_id=(lax.rem(y + k, NY) * NZ + z, me), device_id_type=MESH)
        for k in range(1, NM):
            pl.semaphore_signal(barrier, inc=1, device_id=(dp, lax.rem(me + k, NM)), device_id_type=MESH)

    weights_in.start()

    with jax.named_scope("gelu"):
        x_in.wait()
        cot_in.wait()
        pre = x_ref[...]
        act = 0.5 * pre * (1.0 + lax.erf(pre * 0.7071067811865476))
        ac[me] = act.T
        at[me, 0] = ac[me, pl.ds(pl.multiple_of(8 * z, 8), 8), :]
        cot = cot_ref[...]
        cot_t = jnp.concatenate([cot, jnp.zeros_like(cot)], axis=1).T[:64]
        ct[z] = cot_t

    with jax.named_scope("prepare"):
        weights_in.wait()
        for t in range(TAPS):
            high, low = halves(wv[t])
            wh[64 * t : 64 * t + 64, :] = high
            wl[64 * t : 64 * t + 64, :] = low
        wh[64 * TAPS :, :] = jnp.zeros_like(wh[64 * TAPS :, :])
        wl[64 * TAPS :, :] = jnp.zeros_like(wl[64 * TAPS :, :])
        stack = stacked_taps(cot_t)
        sh[0], sl[0] = halves(stack)
        stack_t = halves(stack.T)
        for m in range(0, NM, 2):
            span = slice(CD * m, CD * m + 2 * CD)
            pair = dot3(stack_t, (wh[:, span], wl[:, span]), NN)
            ig[m] = pair[:, :CD]
            ig[m + 1] = pair[:, CD:]

    with jax.named_scope("barwait"):
        pl.semaphore_wait(barrier, NZ - 1 + NY - 1 + NM - 1)

    def offset(j):
        half = lax.div(j + 1, 2)
        return half * (2 * lax.rem(j, 2) - 1)

    def to_ring(j):
        there = lax.rem(z + offset(j) + NZ, NZ)
        rows = pl.ds(pl.multiple_of(8 * there, 8), 8)
        return remote(ac.at[me, rows], at.at[me, j], za, j, j, y * NZ + there, me)

    def across_x(k):
        return remote(ac.at[me], ac.at[me], acx, k, k, dp, across(k))

    def to_mate(k):
        block = across(-k)
        return remote(ac.at[block], ac.at[block], acp, k, k, dp, mate)

    def part_across_x(p, k):
        part = at.at[me, pl.ds(HALF * p, HALF)]
        return remote(part, part, atx, NX * p + k, NX * p + k, dp, across(k))

    def part_to_mate(p, k):
        part = at.at[across(-k), pl.ds(HALF * p, HALF)]
        return remote(part, part, atp, NX * p + k, NX * p + k, dp, mate)

    RIGHT, LEFT = NZ // 2, NZ // 2 - 1
    TALL = 64 // CHUNKS

    def rightward(s, q):
        part = ct.at[lax.rem(z - s + 1 + NZ, NZ), pl.ds(TALL * q, TALL)]
        return remote(part, part, cr, CHUNKS * s + q, CHUNKS * s + q, ring(1), me)

    def leftward(s, q):
        part = ct.at[lax.rem(z + s - 1, NZ), pl.ds(TALL * q, TALL)]
        return remote(part, part, cl, CHUNKS * s + q, CHUNKS * s + q, ring(-1), me)

    for q in range(CHUNKS):
        rightward(1, q).start()
        leftward(1, q).start()

    def send_channels(first, end):
        @pl.loop(first, end)
        def _(j):
            to_ring(j).start()

    send_channels(1, HALF)

    def mates_share(k):
        return remote(ig.at[2 * k + 1 - c], rp.at[k], rps, k, k, dp, mate)

    for k in range(NX):
        mates_share(k).start()

    def start_part(p):
        @pl.loop(max(1, HALF * p), HALF * (p + 1))
        def _(j):
            to_ring(j).wait_recv()

        for k in range(1, NX):
            part_across_x(p, k).start()
        part_to_mate(p, 0).start()

    def pass_part(p):
        for k in range(1, NX):
            part_across_x(p, k).wait_recv()
            part_to_mate(p, k).start()

    def part_here(p):
        for k in range(NX):
            part_to_mate(p, k).wait_recv()

    def start_activations():
        for k in range(1, NX):
            across_x(k).start()
        to_mate(0).start()

    def pass_activations():
        for k in range(1, NX):
            across_x(k).wait_recv()
            to_mate(k).start()

    def share(k):
        own = across(k)
        return remote(ig.at[own], rx.at[x], rxs, k, k, dp, own)

    def add_shares():
        for k in range(NX):
            mates_share(k).wait_recv()
            ig[2 * k + c] = ig[2 * k + c] + rp[k]

    def start_shares():
        for k in range(1, NX):
            share(k).start()

    def stacks(first, end):
        @pl.loop(first, end)
        def _(j):
            sh[j], sl[j] = halves(stacked_taps(ct[lax.rem(z - offset(j) + NZ, NZ)]))

    def leaves(first, end):
        @pl.loop(first, end)
        def _(j):
            channels = halves(at[:, j].reshape(CG, PIX))
            lt[lax.rem(z - offset(j) + NZ, NZ)] = dot3_joined(channels, (sh[j], sl[j]), NT) * (1.0 / PIX)

    last = CHUNKS - 1
    if NZ == 16:
        plan = {
            (1, 1): [(send_channels, HALF, NZ)],
            (2, 0): [(start_part, 0)],
            (2, 3): [(stacks, 1, 3)],
            (3, 3): [(stacks, 3, 5)],
            (4, 0): [(start_part, 1), (start_activations,)],
            (4, 1): [(pass_part, 0)],
            (4, 3): [(stacks, 5, 7)],
            (5, 3): [(part_here, 0), (leaves, 0, 5), (add_shares,)],
            (6, 1): [(pass_part, 1)],
            (6, 3): [(stacks, 7, 11), (leaves, 5, 8)],
            (7, 3): [(stacks, 11, 15), (part_here, 1), (leaves, 8, 15)],
            (8, 3): [(stacks, 15, 16), (leaves, 15, 16)],
        }
    else:
        plan = {
            (RIGHT, last): [
                (send_channels, HALF, NZ),
                (start_part, 0), (add_shares,), (start_part, 1), (start_activations,),
                (pass_part, 0), (part_here, 0), (pass_part, 1), (part_here, 1), (stacks, 1, NZ), (leaves, 0, NZ),
            ],
        }

    merged = {}
    for (s, q), works in plan.items():
        merged.setdefault((s, q // 2 if NZ == 16 else q), []).extend(works)
    plan = merged

    for s in range(1, RIGHT + 1):
        for q in range(CHUNKS):
            with jax.named_scope(f"wait{s}_{q}"):
                rightward(s, q).wait_recv()
                if s < RIGHT:
                    rightward(s + 1, q).start()
                if s <= LEFT:
                    leftward(s, q).wait_recv()
                    if s < LEFT:
                        leftward(s + 1, q).start()
            for work in plan.get((s, q), []):
                with jax.named_scope(f"{work[0].__name__}{work[1] if len(work) > 1 else 0}"):
                    work[0](*work[1:])

    def exchange(buf, n, mine, sems, device, between=None):
        there = lambda k: lax.rem(mine + k, n)

        @pl.loop(1, n)
        def _(k):
            remote(buf.at[mine], buf.at[mine], sems, k, k, *device(there(k))).start()

        if between is not None:
            between()

        @pl.loop(1, n)
        def _(k):
            remote(buf.at[mine], buf.at[there(n - k)], sems, k, k, *device(there(k))).wait_recv()

        total = buf[0]
        for k in range(1, n):
            total = total + buf[k]
        return total

    def sent(n, buf, mine, sems, device):
        there = lambda k: lax.rem(mine + k, n)

        @pl.loop(1, n)
        def _(k):
            remote(buf.at[mine], buf.at[mine], sems, k, k, *device(there(k))).wait_send()

    on_mp = lambda k: (dp, k)
    on_z = lambda k: (y * NZ + k, me)
    on_y_mp = lambda k: (lax.div(k, NM) * NZ + z, lax.rem(k, NM))

    def share_and_convolve():
        start_shares()
        convolve()

    def convolve():
        for k in range(NX):
            to_mate(k).wait_recv()
        full = halves(ac[...].reshape(NM * CD, PIX))
        total = None
        for t in range(TAPS):
            rows = slice(64 * t, 64 * t + 64)
            product = dot3((wh[rows, :], wl[rows, :]), full, NN)
            moved = shifted(product, t // 3 - 1, t % 3 - 1)
            total = moved if total is None else total + moved
        total = jnp.concatenate([total, jnp.zeros_like(total)], axis=0).T
        out_ref[...] = total[:, :64]

    def finish_shares():
        total = ig[me]
        for k in range(1, NX):
            share(k).wait_recv()
            total = total + rx[lax.rem(x - k + NX, NX)]
        ig_ref[...] = total * gelu_slope(x_ref[...])

    with jax.named_scope("gram16"):
        gm[me] = packed(gram(lt, NZ, CG), NZ)
    with jax.named_scope("g16mp"):
        gz[z] = exchange(gm, NM, me, gms, on_mp, pass_activations)
    with jax.named_scope("g16z"):
        table = exchange(gz, NZ, z, gzs, on_z, share_and_convolve)
    with jax.named_scope("coef16"):
        table = unpacked(table, NZ, cb)
        rows = table.shape[0]
        cb[0:rows, :] = coefficients(table, NZ)
    with jax.named_scope("comb16"):
        total = None
        for i in range(NZ):
            scale = jnp.concatenate([cb[i : i + 1, :]] * (STACK // 128), axis=1)
            term = lt[i] * scale
            total = term if total is None else total + term
        bt[...] = total
        yb[y] = bt[pl.ds(pl.multiple_of(QUARTER * y, 8), QUARTER), :]

    def to_y(k):
        there = lax.rem(y + k, NY)
        rows = pl.ds(pl.multiple_of(QUARTER * there, 8), QUARTER)
        return remote(bt.at[rows], yb.at[y], ys, k, k, there * NZ + z, me)

    with jax.named_scope("ywait"):
        for k in range(1, NY):
            to_y(k).start()
        for k in range(1, NY):
            to_y(k).wait_recv()

    def group(j):
        m, tap = divmod(j, TAPS)
        number = NZ * NM * tap + NZ * ((QUARTER // 8) * y + m) + z
        return lax.div(number, GROUPS), lax.rem(number, GROUPS)

    lower = lax.broadcasted_iota(jnp.int32, (8, 128), 1) < 64

    def send_groups():
        with jax.named_scope("permsend"):
            for j in range(GROUPS):
                m, tap = divmod(j, TAPS)
                span = slice(128 * (tap // 2), 128 * (tap // 2) + 128)
                for h in range(NY // 2):
                    left = yb[2 * h, 8 * m : 8 * m + 8, span]
                    right = yb[2 * h + 1, 8 * m : 8 * m + 8, span]
                    if tap % 2:
                        left = pltpu.roll(left, 64, 1)
                    else:
                        right = pltpu.roll(right, 64, 1)
                    pk[j, 8 * h : 8 * h + 8, :] = jnp.where(lower, left, right)
            for j in range(GROUPS):
                owner, slot = group(j)

                @pl.when(owner != dp)
                def _():
                    remote(pk.at[j], ob.at[slot], ps, j, slot, owner, me).start()

                @pl.when(owner == dp)
                def _():
                    pltpu.make_async_copy(pk.at[j], ob.at[slot], ps.at[1, slot]).start()

    def settle():
        finish_shares()

        @pl.loop(1, NZ)
        def _(j):
            to_ring(j).wait_send()

        for q in range(CHUNKS):
            for s in range(1, RIGHT + 1):
                rightward(s, q).wait_send()
            for s in range(1, LEFT + 1):
                leftward(s, q).wait_send()
        for k in range(NX):
            if k:
                across_x(k).wait_send()
                share(k).wait_send()
                for p in range(2):
                    part_across_x(p, k).wait_send()
            to_mate(k).wait_send()
            mates_share(k).wait_send()
            for p in range(2):
                part_to_mate(p, k).wait_send()
        for k in range(1, NY):
            to_y(k).wait_send()
        sent(NM, gm, me, gms, on_mp)
        sent(NZ, gz, z, gzs, on_z)

    with jax.named_scope("gram4"):
        here = NM * y + me
        hm[here] = packed(gram(yb, NY, QUARTER), NY)
    with jax.named_scope("g4ymp"):
        hz[z] = exchange(hm, NY * NM, here, hms, on_y_mp, send_groups)
    with jax.named_scope("g4z"):
        table = exchange(hz, NZ, z, hzs, on_z, settle)
    with jax.named_scope("coef4"):
        table = unpacked(table, NY, cb)
        cb[0:8, :] = coefficients(table, NY)
        scales = [jnp.where(lower, cb[2 * h : 2 * h + 1, :], cb[2 * h + 1 : 2 * h + 2, :]) for h in range(NY // 2)]
    with jax.named_scope("permrecv"):
        pieces = []
        for s in range(GROUPS):
            pltpu.make_async_copy(ob.at[s], ob.at[s], ps.at[1, s]).wait()
            piece = None
            for h in range(NY // 2):
                term = ob[s, 8 * h : 8 * h + 8, :] * scales[h]
                piece = term if piece is None else piece + term
            pieces.append(piece)
        columns = jnp.concatenate(pieces, axis=0)
        columns = columns + pltpu.roll(columns, 64, 1)
        fill = -8 * GROUPS % 128
        columns = jnp.concatenate([columns, jnp.zeros((fill, 128), F32)], axis=0).T
        wg_ref[...] = columns[:64, : 8 * GROUPS]

    with jax.named_scope("drain"):
        sent(NY * NM, hm, here, hms, on_y_mp)
        sent(NZ, hz, z, hzs, on_z)
        for j in range(GROUPS):
            owner, slot = group(j)

            @pl.when(owner != dp)
            def _():
                remote(pk.at[j], ob.at[slot], ps, j, slot, owner, me).wait_send()


def local(NY, NZ, NX, preact, weights, cotangent):
    NM = 2 * NX
    CD = preact.shape[3]
    CG = 8 * NM
    QUARTER = CG // NY
    GROUPS = TAPS * NM // NY
    rows16 = NZ // min(NZ, 128 // NZ)
    vmem = lambda *shape: pltpu.VMEM(shape, F32)
    sems = lambda n: pltpu.SemaphoreType.DMA((2, n))
    anywhere = pl.BlockSpec(memory_space=pl.ANY)
    output, input_grad, weight_grad = pl.pallas_call(
        functools.partial(kernel, NY, NZ, NX),
        out_shape=[
            jax.ShapeDtypeStruct((PIX, 64), F32),
            jax.ShapeDtypeStruct((PIX, CD), F32),
            jax.ShapeDtypeStruct((64, 8 * GROUPS), F32),
        ],
        in_specs=[anywhere] * 3,
        out_specs=[pl.BlockSpec(memory_space=pltpu.VMEM)] * 3,
        scratch_shapes=[
            vmem(PIX, CD),
            vmem(PIX, 64),
            vmem(TAPS, 64, NM * CD),
            pltpu.VMEM((STACK, NM * CD), BF16),
            pltpu.VMEM((STACK, NM * CD), BF16),
            vmem(NM, CD, PIX),
            vmem(NM, NZ, 8, PIX),
            vmem(NZ, 64, PIX),
            vmem(NM, PIX, CD),
            vmem(NX, PIX, CD),
            vmem(NX, PIX, CD),
            pltpu.VMEM((NZ, STACK, PIX), BF16),
            pltpu.VMEM((NZ, STACK, PIX), BF16),
            vmem(NZ, CG, STACK),
            vmem(16, 128),
            vmem(CG, STACK),
            vmem(NY, QUARTER, STACK),
            vmem(GROUPS, 4 * NY, 128),
            vmem(GROUPS, 4 * NY, 128),
            vmem(NM, rows16, 128),
            vmem(NZ, rows16, 128),
            vmem(NY * NM, 1, 128),
            vmem(NZ, 1, 128),
            pltpu.SemaphoreType.DMA((3,)),
            sems(NZ), sems(CHUNKS * NZ), sems(CHUNKS * NZ),
            sems(NX), sems(NX), sems(2 * NX), sems(2 * NX), sems(NX), sems(NX),
            sems(NM), sems(NZ), sems(NY), sems(NY * NM), sems(NZ),
            sems(GROUPS),
        ],
        compiler_params=pltpu.CompilerParams(collective_id=0, has_side_effects=True, vmem_limit_bytes=LIMIT),
        name="step",
    )(*(pltpu.with_memory_space_constraint(v, pltpu.HBM) for v in (preact.reshape(PIX, CD), cotangent.reshape(PIX, 64), weights.transpose(1, 0, 2))))
    def hand_over(a, b, d, e, f, g):
        e[...] = a[...]
        f[...] = b[...]
        g[...] = d[...]

    whole = pl.BlockSpec(memory_space=pltpu.VMEM)
    output, input_grad, weight_grad = pl.pallas_call(
        hand_over,
        out_shape=[jax.ShapeDtypeStruct(v.shape, F32) for v in (output, input_grad, weight_grad)],
        in_specs=[whole] * 3,
        out_specs=[whole] * 3,
        compiler_params=pltpu.CompilerParams(vmem_limit_bytes=2 * 2**20),
        name="hand_over",
    )(output, input_grad, weight_grad)
    return output.reshape(1, SIDE, SIDE, 64), input_grad.reshape(preact.shape), weight_grad


def build(mesh, NY, NZ, NX):
    placed = (P("dp", None, None, "mp"), P("mp", None, None), P("dp", None, None, "mp"))
    return jax.shard_map(
        functools.partial(local, NY, NZ, NX),
        mesh=mesh,
        in_specs=placed,
        out_specs=(P("dp", None, None, "mp"), P("dp", None, None, "mp"), P("mp", "dp")),
        check_vma=False,
    )


def solution(mesh):
    return build(mesh, 4, mesh.shape["dp"] // 4, mesh.shape["mp"] // 2)
```
